512 devices in a mesh: row: 4 (over x), col: 16 (over y_lo, z), aux: 8 (over y_hi, core).
Axes of the slice: x: 4, y: 8 (y_hi: 4, y_lo: 2; y = y_hi * 2 + y_lo), z: 8, core: 2. Of those that a mesh axis runs over, the one named last changes fastest.
Arguments:
- green_occ: bfloat16 [4096, 4096], P('row', 'col'), may hold values from -6 to 6
- green_virt: bfloat16 [4096, 4096], P('row', 'col'), may hold values from -0.09375 to 0.09375
- integrals: bfloat16 [4, 16, 256, 8, 4096], P('row', 'col', 'aux'), may hold values from -0.0625 to 0.0625
- listed_tile_index: int32 [4, 16, 8, 8], P('row', 'col', 'aux'), may hold values from 0 to 63, as said below
- metric: float32 [256, 256], P('aux'), may hold values from -0.375 to 0.375
Outputs:
- product: bfloat16 [4096, 4096], P('row', 'col')
- aux_coeff: float32 [256], P('aux')
- occ_force: float32 [4096, 4096], P('col', ('row', 'aux'))
The draws below stay inside these ranges and needn't reach their ends.
Inputs may be any that keep to these rules, and one draw needn't show every extreme that they name: Each entry of listed_tile_index[r, c, a] is a distinct tile of tile (r, c). Aux owner o holds block rows o * 2 to (o + 1) * 2 - 1 of every tile; each list names exactly 2 tiles in each of 4 owners and none in the others. In every tile (r, c) one owner receives 2 tiles from every aux index.
All inputs are finite; a program needn't handle non-finite values.
Results may differ from the reference program's by a relative error of at most 0.0048.
Values may be sent and summed in bfloat16 or wider, within the bound.
A program may use at most 64 MiB of HBM per device.

```python
import jax
import jax.numpy as jnp
from jax import lax

BLK = 64
AUX_DEV = 32
CAP = 2
NAO = 4096
NAUX = 256
TR = 16
TC = 4
NNZ = 8
N_ROW = 4
N_COL = 16
N_AUX = 8


def draw_listed_tile_index(key, part):
    owners_used = NNZ // CAP
    owner_tiles = TR // N_AUX * TC
    key_hot, key_owner, key_tile = jax.random.split(key, 3)
    hottest = jax.random.randint(key_hot, (N_ROW, N_COL, 1, 1), 0, N_AUX)
    owner_keys = jax.random.split(key_owner, N_ROW * N_COL * N_AUX)
    shuffled = jax.vmap(lambda k: jax.random.permutation(k, N_AUX - 1))(owner_keys)
    shuffled = shuffled.reshape(N_ROW, N_COL, N_AUX, N_AUX - 1)[..., :owners_used - 1]
    others = shuffled + (shuffled >= hottest).astype(jnp.int32)
    owner_devices = jnp.concatenate([jnp.broadcast_to(hottest, (N_ROW, N_COL, N_AUX, 1)), others], axis=-1)
    tile_keys = jax.random.split(key_tile, N_ROW * N_COL * N_AUX * owners_used)
    picks = jax.vmap(lambda k: jax.random.permutation(k, owner_tiles)[:CAP])(tile_keys)
    picks = picks.reshape(N_ROW, N_COL, N_AUX, owners_used, CAP)
    listed = owner_devices[..., None] * owner_tiles + picks
    return listed.reshape(N_ROW, N_COL, N_AUX, NNZ).astype(jnp.int32)


def shard_levels(key, dims, cuts, least, high):
    def one(axis_at, parts):
        draws = jax.random.uniform(jax.random.fold_in(jax.random.fold_in(key, 6), axis_at), (parts,), jnp.float32, least / len(cuts), high / len(cuts))
        return jnp.repeat(jnp.exp(draws), dims[axis_at] // parts).reshape((-1,) + (1,) * (len(dims) - axis_at - 1))

    level = one(*cuts[0])
    for cut in cuts[1:]:
        level = level * one(*cut)
    return level


def scatter_about(rng, dims, width, most, cuts=(), held_as=jnp.bfloat16):
    array = width * jax.random.normal(rng, dims, jnp.float32)
    if cuts:
        array = array * shard_levels(rng, dims, cuts, -0.22, 0.18)
    return jnp.clip(array, -most, most).astype(held_as)


def setup_inputs(seed: int = 0) -> dict:
    key_of = jax.random.split(jax.random.key(seed), 6)
    green_occ = scatter_about(key_of[0], (NAO, NAO), 1.0, 6.0, ((0, 4), (1, 16)))
    green_virt = scatter_about(key_of[1], (NAO, NAO), NAO ** -0.5, 0.09375, ((0, 4), (1, 16)))
    integrals = scatter_about(key_of[2], (N_ROW, N_COL, NAUX, NNZ, BLK * BLK), (2 * BLK * BLK) ** -0.5, 0.0625, ((0, 4), (1, 16), (2, 8)))
    listed_tile_index = draw_listed_tile_index(jax.random.fold_in(key_of[5], 71), 0)
    metric = scatter_about(key_of[4], (NAUX, NAUX), NAUX ** -0.5, 0.375, ((0, 8),), jnp.float32)
    return dict(green_occ=green_occ, green_virt=green_virt, integrals=integrals, listed_tile_index=listed_tile_index, metric=metric)


def reference(green_occ, green_virt, integrals, listed_tile_index, metric):
    product = jnp.dot(green_occ, green_virt, preferred_element_type=jnp.float32).astype(jnp.bfloat16)
    tiles = product.reshape(N_ROW, TR, BLK, N_COL, TC, BLK).transpose(0, 3, 1, 4, 2, 5)
    tiles = tiles.reshape(N_ROW * N_COL, TR * TC, BLK * BLK)
    lists = listed_tile_index.reshape(N_ROW * N_COL, N_AUX, NNZ).astype(jnp.int32)
    local_ints = integrals.reshape(N_ROW * N_COL, N_AUX, AUX_DEV, NNZ, BLK * BLK)

    def contract(items):
        tile_set, listed, local = items
        chosen = jnp.take(tile_set, listed.reshape(-1), axis=0).reshape(N_AUX, NNZ, BLK * BLK).astype(jnp.float32)
        return jnp.einsum("apnk,ank->ap", local.astype(jnp.float32), chosen, precision=lax.Precision.HIGHEST)

    aux_coeff = jnp.sum(lax.map(contract, (tiles, lists, local_ints)), axis=0).reshape(NAUX)
    screened_blocks = jnp.dot(metric, aux_coeff, precision=lax.Precision.HIGHEST).reshape(N_AUX, AUX_DEV)

    def spread_values(items):
        listed, local = items
        block_values = jnp.einsum("ap,apnk->ank", screened_blocks, local.astype(jnp.float32), precision=lax.Precision.HIGHEST)
        owner_indicator = (listed[:, :, None] == jnp.arange(TR * TC, dtype=jnp.int32)[None, None, :]).astype(jnp.float32)
        return jnp.einsum("iyc,iyx->cx", owner_indicator, block_values, precision=lax.Precision.HIGHEST)

    dense = lax.map(spread_values, (lists, local_ints)).astype(jnp.bfloat16)
    derivative = dense.reshape(N_ROW, N_COL, TR, TC, BLK, BLK).transpose(0, 2, 4, 1, 3, 5).reshape(NAO, NAO)
    occ_force = jnp.dot(green_virt, derivative.T, preferred_element_type=jnp.float32)
    return product, aux_coeff, occ_force
```

```python
import jax
import jax.numpy as jnp
from jax import lax
from jax.experimental import pallas as pl
from jax.experimental.pallas import tpu as pltpu
from jax.sharding import Mesh
from jax.sharding import PartitionSpec as P

MESH = pl.DeviceIdType.MESH
BF = jnp.bfloat16
F32 = jnp.float32
NX, NYL, NZ, NYH, NCO = 4, 2, 8, 4, 2
NCOPY = 144


def iota(shape, dim):
    return lax.broadcasted_iota(jnp.int32, shape, dim)


def rows_from_tiles(fl, rows):
    left = iota((32, 128), 1) < 64
    for br in range(2):
        for q in range(2):
            t = br * 4 + 2 * q
            a = fl[pl.ds(t, 32, stride=8), :]
            b = fl[pl.ds(t + 1, 32, stride=8), :]
            even = jnp.where(left, a, pltpu.roll(b, 64, 1))
            odd = jnp.where(left, pltpu.roll(a, 64, 1), b)
            rows[q, pl.ds(br * 64, 32, stride=2), :] = even
            rows[q, pl.ds(br * 64 + 1, 32, stride=2), :] = odd


def tiles_from_rows(rows, fl):
    left = iota((32, 128), 1) < 64
    for br in range(2):
        for q in range(2):
            t = br * 4 + 2 * q
            even = rows[q, pl.ds(br * 64, 32, stride=2), :]
            odd = rows[q, pl.ds(br * 64 + 1, 32, stride=2), :]
            fl[pl.ds(t, 32, stride=8), :] = jnp.where(left, even, pltpu.roll(odd, 64, 1))
            fl[pl.ds(t + 1, 32, stride=8), :] = jnp.where(left, pltpu.roll(even, 64, 1), odd)


def body(
    listed, occ, virt, ints, metric, prod_out, coeff_out, force_out,
    VIRT, OCC, AV, FL, ROWS, TILES, TF, CSRC, CZ, CX, CY, ACC, SCB, LSRC, LB,
    BV, SB, RB, FP, SH, RH, SF, RF, SY, RY, SP, RP, ssem, rsem, lsem,
):
    x = lax.axis_index("row")
    yl = lax.axis_index("ylo")
    z = lax.axis_index("z")
    yh = lax.axis_index("yhi")
    co = lax.axis_index("core")
    a = yh * 2 + co
    count = [0]
    started = []

    def send(src, dst, **to):
        k = count[0]
        count[0] += 1
        c = pltpu.make_async_remote_copy(
            src_ref=src, dst_ref=dst, send_sem=ssem.at[k], recv_sem=rsem.at[k],
            device_id=to, device_id_type=MESH,
        )
        c.start()
        started.append(c)
        return c

    def shift(axis, n, me, d):
        return {axis: lax.rem(me + d + n, n)}

    def ypeers():
        for dl in range(NYL):
            for dh in range(NYH):
                for dc in range(NCO):
                    if dl or dh or dc:
                        yield {
                            "ylo": lax.rem(yl + dl, NYL),
                            "yhi": lax.rem(yh + dh, NYH),
                            "core": lax.rem(co + dc, NCO),
                        }

    partner = {"core": 1 - co}
    ypair = {"ylo": 1 - yl}

    local = [
        pltpu.make_async_copy(virt, VIRT.at[pl.ds(x * 1024, 1024)], lsem.at[0]),
        pltpu.make_async_copy(occ.at[pl.ds(a * 128, 128)], OCC.at[yl * 8 + z], lsem.at[1]),
        pltpu.make_async_copy(ints, AV, lsem.at[2]),
    ]
    for c in local:
        c.start()

    barrier = pltpu.get_barrier_semaphore()
    peers = [shift("row", NX, x, d) for d in range(1, NX)]
    peers += [shift("z", NZ, z, d) for d in range(1, NZ)]
    peers += list(ypeers())
    for p in peers:
        pl.semaphore_signal(barrier, inc=1, device_id=p, device_id_type=MESH)
    pl.semaphore_wait(barrier, len(peers))

    def vq(r, half, quarter):
        return VIRT.at[pl.ds(r * 1024 + half * 512 + quarter * 256, 256)]

    def own_vq(quarter):
        return virt.at[pl.ds(co * 512 + quarter * 256, 256)]

    def xblk(d):
        return lax.rem(x + d + NX, NX)

    def occ_rows(c, r0, n):
        return OCC.at[c, pl.ds(r0, n)]

    def own_occ(r0, n):
        return occ.at[pl.ds(a * 128 + r0, n)]

    def zat(d):
        return lax.rem(z + d + NZ, NZ)

    SIGN = {"+": 1, "-": -1}
    xs = {}
    for d, order in (("+", (0, 1)), ("-", (1, 0))):
        xs[d] = [
            send(own_vq(q), vq(x, co, q), **shift("row", NX, x, SIGN[d])) for q in order
        ]
    ya = send(own_occ(0, 64), occ_rows(yl * 8 + z, 0, 64), **ypair)
    za = {}
    for name, r0 in (("A", 0), ("B", 64)):
        for d in "+-":
            za[name, d, 1] = send(
                own_occ(r0, 64), occ_rows(yl * 8 + z, r0, 64), **shift("z", NZ, z, SIGN[d])
            )
    yb = [send(own_occ(64, 64), occ_rows(yl * 8 + z, 64, 64), **ypair)]

    lane = iota((8, 128), 1)
    subl = iota((8, 128), 0)
    idx = [listed[0, n] for n in range(8)]
    own = [lax.shift_right_logical(v, 3) for v in idx]
    pos = [jnp.bitwise_and(v, 7) for v in idx]
    rank = []
    for n in range(8):
        r = jnp.int32(0)
        for m in range(n):
            r = r + jnp.where(own[m] == own[n], 1, 0).astype(jnp.int32)
        rank.append(r)
    table = jnp.zeros((8, 128), F32)
    for n in range(8):
        hit = (subl == own[n]) & (lane // 4 == a * 2 + rank[n])
        table = table + jnp.where(hit, (pos[n] + 1).astype(F32), 0.0)
    LSRC[...] = table
    LB[a] = table
    lab = []
    for dh in range(NYH):
        for dc in range(NCO):
            if dh or dc:
                lab.append(
                    send(LSRC, LB.at[a], yhi=lax.rem(yh + dh, NYH), core=lax.rem(co + dc, NCO))
                )

    ya.wait_recv()
    for d in "+-":
        c = (1 - yl) * 8 + z
        za["P", d, 1] = send(occ_rows(c, 0, 64), occ_rows(c, 0, 64), **shift("z", NZ, z, SIGN[d]))

    def relay(name, d, step):
        s = SIGN[d]
        r0 = 64 if name == "B" else 0
        c = ((1 - yl) if name == "P" else yl) * 8 + zat(-s * step)
        za[name, d, step].wait_recv()
        if step <= 2:
            za[name, d, step + 1] = send(
                occ_rows(c, r0, 64), occ_rows(c, r0, 64), **shift("z", NZ, z, s)
            )
        elif step == 3:
            h0 = r0 + (0 if d == "+" else 32)
            za[name, d, 4] = send(
                occ_rows(c, h0, 32), occ_rows(c, h0, 32), **shift("z", NZ, z, s)
            )
        if name == "B" and step <= 3:
            yb.append(send(occ_rows(c, 64, 64), occ_rows(c, 64, 64), **ypair))

    def zstep(step):
        for name in ("A", "B", "P"):
            for d in "+-":
                relay(name, d, step)
        if step == 4:
            c = yl * 8 + zat(4)
            yb.append(send(occ_rows(c, 64, 64), occ_rows(c, 64, 64), **ypair))

    fwd = []

    def xfwd(r, q):
        fwd.append(send(vq(r, co, q), vq(r, co, q), **partner))

    zstep(1)
    for d, q in (("+", 0), ("-", 1)):
        s = SIGN[d]
        xs[d][0].wait_recv()
        r = xblk(-s)
        xs[d].append(send(vq(r, co, q), vq(r, co, q), **shift("row", NX, x, s)))
        xfwd(r, q)
    zstep(2)
    for d, q in (("+", 1), ("-", 0)):
        xs[d][1].wait_recv()
        xfwd(xblk(-SIGN[d]), q)
    zstep(3)
    for d, q in (("+", 0), ("-", 1)):
        xs[d][2].wait_recv()
        xfwd(xblk(2), q)
    zstep(4)
    for c in local:
        c.wait()
    for c in fwd:
        c.wait_recv()
    for c in yb:
        c.wait_recv()

    def mm(c, acc):
        return acc + jnp.dot(
            OCC[c], VIRT[pl.ds(pl.multiple_of(c * 256, 256), 256), :], preferred_element_type=F32
        )

    acc = lax.fori_loop(0, NYL * NZ, mm, jnp.zeros((128, 256), F32), unroll=4)
    for q in range(2):
        ROWS[q] = acc[:, q * 128 : (q + 1) * 128]
    tiles_from_rows(ROWS, FL)
    for m in range(32):
        TILES[a, :, m * 128 : (m + 1) * 128] = FL[m * 8 : (m + 1) * 8, :].astype(BF)

    def th(o, h):
        return TILES.at[o, :, pl.ds(h * 2048, 2048)]

    core_own = send(TILES.at[a], TILES.at[a], **partner)
    ts = {}
    for d, order in (("+", (0, 1)), ("-", (1, 0))):
        ts[d] = [send(th(a, h), th(a, h), **shift("yhi", NYH, yh, SIGN[d])) for h in order]
    tf = []

    def own_at(d):
        return lax.rem(yh + d + NYH, NYH) * 2 + co

    def tfwd(o, h):
        tf.append(send(th(o, h), th(o, h), **partner))

    for d, h in (("+", 0), ("-", 1)):
        s = SIGN[d]
        ts[d][0].wait_recv()
        o = own_at(-s)
        ts[d].append(send(th(o, h), th(o, h), **shift("yhi", NYH, yh, s)))
        tfwd(o, h)
    for d, h in (("+", 1), ("-", 0)):
        ts[d][1].wait_recv()
        tfwd(own_at(-SIGN[d]), h)
    for d, h in (("+", 0), ("-", 1)):
        ts[d][2].wait_recv()
        tfwd(own_at(2), h)
    core_own.wait_recv()
    for c in tf:
        c.wait_recv()

    for o in range(8):
        TF[o * 8 : (o + 1) * 8, :] = TILES[o].astype(F32)
    s64 = iota((8, 64), 1)
    n64 = iota((8, 64), 0)
    pick = jnp.zeros((8, 64), F32)
    for n in range(8):
        pick = pick + jnp.where((n64 == n) & (s64 == idx[n]), 1.0, 0.0)
    chosen = jnp.dot(pick.astype(BF), TF[...].astype(BF), preferred_element_type=F32)

    def contract(p, _):
        v = AV[p].astype(F32) * chosen
        s = v[:, 0:128]
        for m in range(1, 32):
            s = s + v[:, m * 128 : (m + 1) * 128]
        ACC[p] = s
        return 0

    lax.fori_loop(0, 32, contract, 0, unroll=2)
    part = jnp.sum(jnp.sum(ACC[...], axis=1), axis=1, keepdims=True)
    lane32 = iota((32, 128), 1)
    sub32 = iota((32, 128), 0)
    spread = jnp.where(lane32 == sub32 + lax.rem(a, 4) * 32, part, 0.0)
    spread = jnp.sum(spread, axis=0, keepdims=True)
    coeff = jnp.where(subl == a // 4, jnp.broadcast_to(spread, (8, 128)), 0.0)

    def exchange(k, value, buf, slot, targets, n, between=None):
        CSRC[k] = value
        buf[slot] = value
        cs = [send(CSRC.at[k], buf.at[slot], **t) for t in targets]
        if between is not None:
            between()
        for c in cs:
            c.wait_recv()
        total = buf[0]
        for i in range(1, n):
            total = total + buf[i]
        return total

    def write_product():
        def one(o, _):
            for m in range(32):
                FL[m * 8 : (m + 1) * 8, :] = TF[
                    pl.ds(pl.multiple_of(o * 8, 8), 8), m * 128 : (m + 1) * 128
                ]
            rows_from_tiles(FL, ROWS)
            for q in range(2):
                prod_out[pl.ds(pl.multiple_of(o * 128, 128), 128), q * 128 : (q + 1) * 128] = ROWS[
                    q
                ].astype(BF)
            return 0

        lax.fori_loop(0, 8, one, 0)

    coeff = exchange(
        0, coeff, CZ, z, [shift("z", NZ, z, d) for d in range(1, NZ)], NZ, write_product
    )
    coeff = exchange(1, coeff, CX, x, [shift("row", NX, x, d) for d in range(1, NX)], NX)
    coeff = exchange(2, coeff, CY, yl * 8 + a, list(ypeers()), 16)

    row = jnp.sum(jnp.where(subl == a // 4, coeff, 0.0), axis=0, keepdims=True)
    mine = jnp.zeros((1, 32), F32)
    for k in range(4):
        mine = mine + jnp.where(lax.rem(a, 4) == k, row[:, k * 32 : (k + 1) * 32], 0.0)
    coeff_out[...] = mine

    scr = metric[:, 0:128] * coeff[0:1, :] + metric[:, 128:256] * coeff[1:2, :]
    scr = jnp.sum(scr, axis=1, keepdims=True)
    SCB[...] = jnp.broadcast_to(scr, (32, 128))

    def weigh(p, accs):
        s = SCB[pl.ds(p, 1), :]
        v = AV[p].astype(F32)
        return tuple(accs[m] + v[:, m * 128 : (m + 1) * 128] * s for m in range(32))

    accs = lax.fori_loop(
        0, 32, weigh, tuple(jnp.zeros((8, 128), F32) for _ in range(32))
    )
    for m in range(32):
        BV[:, m * 128 : (m + 1) * 128] = accs[m]
    i64 = iota((64, 8), 0)
    n8 = iota((64, 8), 1)
    out = jnp.zeros((64, 1024), F32)
    for q in range(4):
        sel = jnp.zeros((64, 8), F32)
        for n in range(8):
            hit = (n8 == n) & (i64 == own[n] * 8 + rank[n] * 4 + q)
            sel = sel + jnp.where(hit, 1.0, 0.0)
        out = out + jnp.dot(
            sel.astype(BF), BV[:, q * 1024 : (q + 1) * 1024].astype(BF), preferred_element_type=F32
        )
    for o in range(8):
        SB[o] = out[o * 8 : (o + 1) * 8, :].astype(BF)
    keep = pltpu.make_async_copy(SB.at[a], RB.at[a], lsem.at[3])
    keep.start()
    ex = []
    for dh in range(NYH):
        for dc in range(NCO):
            if dh or dc:
                h2 = lax.rem(yh + dh, NYH)
                c2 = lax.rem(co + dc, NCO)
                ex.append(send(SB.at[h2 * 2 + c2], RB.at[a], yhi=h2, core=c2))
    for c in lab:
        c.wait_recv()
    labels = LB[0]
    for o in range(1, 8):
        labels = labels + LB[o]
    labels = jnp.sum(jnp.where(subl == a, labels, 0.0), axis=0, keepdims=True)[:, 0:64]
    t64 = iota((8, 64), 0).astype(F32)
    q64 = jnp.bitwise_and(iota((8, 64), 1), 3)
    keep.wait()
    for c in ex:
        c.wait_recv()
    arrived = jnp.concatenate([RB[o].astype(F32) for o in range(8)], axis=0).astype(BF)
    for q in range(4):
        place = jnp.where((labels == t64 + 1.0) & (q64 == q), 1.0, 0.0).astype(BF)
        d = jnp.dot(place, arrived, preferred_element_type=F32)
        for m in range(8):
            FL[(q * 8 + m) * 8 : (q * 8 + m + 1) * 8, :] = d[:, m * 128 : (m + 1) * 128]
    rows_from_tiles(FL, ROWS)
    deriv = jnp.concatenate([ROWS[0], ROWS[1]], axis=1).astype(BF)

    def partial(i, _):
        FP[i] = lax.dot_general(
            VIRT[pl.ds(pl.multiple_of(i * 256, 256), 256), :], deriv,
            (((1,), (1,)), ((), ())), preferred_element_type=F32,
        )
        return 0

    lax.fori_loop(0, 16, partial, 0, unroll=2)

    mycol = yl * 8
    other = (1 - yl) * 8
    order = [4, 3, -3, 2, -2, 1, -1, 0]
    ys = {}
    for k, d in enumerate(order):
        SY[k] = FP[other + zat(d), 128:256, :].astype(BF)
        ys[d] = send(SY.at[k], RY.at[k], **ypair)
    ys[-4] = ys[4]
    YI = {d: k for k, d in enumerate(order)}
    items = {"A": (mycol, 0), "P": (other, 0), "B": (mycol, 128)}
    IX = {"A": 0, "P": 1, "B": 2}
    DX = {"+": 0, "-": 1}
    rs = {}
    added = set()

    def ring(name, d, step):
        base, r0 = items[name]
        i, j, s = IX[name], DX[d], SIGN[d]
        dist = s * (5 - step)
        dest = zat(dist)
        if step > 1:
            rs[name, d, step - 1].wait_recv()
        if name == "B":
            key = 4 if abs(dist) == 4 else dist
            if key not in added:
                added.add(key)
                ys[key].wait_recv()
        extra = YI[4 if abs(dist) == 4 else dist]
        to = shift("z", NZ, z, s)
        if step == 1:
            h0 = 0 if d == "+" else 64
            v = FP[base + dest, r0 + h0 : r0 + h0 + 64, :]
            if name == "B":
                v = v + RY[extra, h0 : h0 + 64, :].astype(F32)
            SH[i, j] = v.astype(BF)
            rs[name, d, 1] = send(SH.at[i, j], RH.at[i, j], **to)
            return
        v = FP[base + dest, r0 : r0 + 128, :]
        if name == "B":
            v = v + RY[extra].astype(F32)
        if step == 2:
            h0 = 0 if d == "+" else 64
            got = RH[i, j].astype(F32)
            zero = jnp.zeros((64, 128), F32)
            v = v + jnp.concatenate([got, zero] if d == "+" else [zero, got], axis=0)
        else:
            v = v + RF[i, j, step - 3].astype(F32)
        SF[i, j, step - 2] = v.astype(BF)
        rs[name, d, step] = send(SF.at[i, j, step - 2], RF.at[i, j, step - 2], **to)

    for step in range(1, 5):
        for name in ("P", "A", "B"):
            for d in "+-":
                ring(name, d, step)

    def final(name):
        base, r0 = items[name]
        i = IX[name]
        v = FP[base + z, r0 : r0 + 128, :]
        for d in "+-":
            rs[name, d, 4].wait_recv()
            v = v + RF[i, DX[d], 2].astype(F32)
        return v

    SP[...] = final("P").astype(BF)
    yp = send(SP, RP, **ypair)
    va = final("A")
    ys[0].wait_recv()
    force_out[128:256, :] = final("B") + RY[YI[0]].astype(F32)
    yp.wait_recv()
    force_out[0:128, :] = va + RP[...].astype(F32)
    for c in started:
        c.wait_send()
    assert count[0] <= NCOPY


def on_device(green_occ, green_virt, integrals, listed, metric):
    vm = pltpu.VMEM
    hbm = pl.BlockSpec(memory_space=pl.ANY)
    inv = pl.BlockSpec(memory_space=pltpu.VMEM)
    product, coeff, force = pl.pallas_call(
        body,
        out_shape=(
            jax.ShapeDtypeStruct((1024, 256), BF),
            jax.ShapeDtypeStruct((1, 32), F32),
            jax.ShapeDtypeStruct((256, 128), F32),
        ),
        in_specs=[pl.BlockSpec(memory_space=pltpu.SMEM), hbm, hbm, hbm, inv],
        out_specs=(inv, inv, inv),
        scratch_shapes=[
            vm((4096, 256), BF),
            vm((16, 128, 256), BF),
            vm((32, 8, 4096), BF),
            vm((256, 128), F32),
            vm((2, 128, 128), F32),
            vm((8, 8, 4096), BF),
            vm((64, 4096), F32),
            vm((3, 8, 128), F32),
            vm((8, 8, 128), F32),
            vm((4, 8, 128), F32),
            vm((16, 8, 128), F32),
            vm((32, 8, 128), F32),
            vm((32, 128), F32),
            vm((8, 128), F32),
            vm((8, 8, 128), F32),
            vm((8, 4096), F32),
            vm((8, 8, 1024), BF),
            vm((8, 8, 1024), BF),
            vm((16, 256, 128), F32),
            vm((3, 2, 64, 128), BF),
            vm((3, 2, 64, 128), BF),
            vm((3, 2, 3, 128, 128), BF),
            vm((3, 2, 3, 128, 128), BF),
            vm((8, 128, 128), BF),
            vm((8, 128, 128), BF),
            vm((128, 128), BF),
            vm((128, 128), BF),
            pltpu.SemaphoreType.DMA((NCOPY,)),
            pltpu.SemaphoreType.DMA((NCOPY,)),
            pltpu.SemaphoreType.DMA((4,)),
        ],
        compiler_params=pltpu.CompilerParams(
            collective_id=0, has_side_effects=True, vmem_limit_bytes=40 << 20
        ),
        name="force_window",
    )(
        listed.reshape(1, 8), green_occ, green_virt, integrals.reshape(32, 8, 4096), metric
    )
    return product, coeff.reshape(32), force


def solution(mesh):
    split = Mesh(
        mesh.devices.reshape(NX, NYL, NZ, NYH, NCO), ("row", "ylo", "z", "yhi", "core")
    )
    col, aux = ("ylo", "z"), ("yhi", "core")
    return jax.shard_map(
        on_device,
        mesh=split,
        in_specs=(
            P("row", col),
            P("row", col),
            P("row", col, aux, None, None),
            P("row", col, aux, None),
            P(aux, None),
        ),
        out_specs=(P("row", col), P(aux), P(col, ("row", *aux))),
        check_vma=False,
    )
```

```python
import jax
import jax.numpy as jnp
from jax import lax
from jax.experimental import pallas as pl
from jax.experimental.pallas import tpu as pltpu
from jax.sharding import Mesh
from jax.sharding import PartitionSpec as P

MESH = pl.DeviceIdType.MESH
BF = jnp.bfloat16
F32 = jnp.float32
NX, NYL, NZ, NYH, NCO = 4, 2, 8, 4, 2
NCOPY = 160


def iota(shape, dim):
    return lax.broadcasted_iota(jnp.int32, shape, dim)


def rows_from_tiles(fl, rows):
    left = iota((32, 128), 1) < 64
    for br in range(2):
        for q in range(2):
            t = br * 4 + 2 * q
            a = fl[pl.ds(t, 32, stride=8), :]
            b = fl[pl.ds(t + 1, 32, stride=8), :]
            even = jnp.where(left, a, pltpu.roll(b, 64, 1))
            odd = jnp.where(left, pltpu.roll(a, 64, 1), b)
            rows[q, pl.ds(br * 64, 32, stride=2), :] = even
            rows[q, pl.ds(br * 64 + 1, 32, stride=2), :] = odd


def tiles_from_rows(rows, fl):
    left = iota((32, 128), 1) < 64
    for br in range(2):
        for q in range(2):
            t = br * 4 + 2 * q
            even = rows[q, pl.ds(br * 64, 32, stride=2), :]
            odd = rows[q, pl.ds(br * 64 + 1, 32, stride=2), :]
            fl[pl.ds(t, 32, stride=8), :] = jnp.where(left, even, pltpu.roll(odd, 64, 1))
            fl[pl.ds(t + 1, 32, stride=8), :] = jnp.where(left, pltpu.roll(even, 64, 1), odd)


def body(
    listed, occ, virt, ints, metric, prod_out, coeff_out, force_out,
    VIRT, OCC, AV, FL, ROWS, PR, CSRC, CZX, CY, ACC, SCB, LSRC, LB,
    BV, SB, RB, ST, RT, FP, S4, R4, S3, R3, S2, R2, S1, R1, SY, RY, ssem, rsem, lsem,
):
    x = lax.axis_index("row")
    yl = lax.axis_index("ylo")
    z = lax.axis_index("z")
    yh = lax.axis_index("yhi")
    co = lax.axis_index("core")
    a = yh * 2 + co
    count = [0]
    started = []

    def send(src, dst, **to):
        k = count[0]
        count[0] += 1
        c = pltpu.make_async_remote_copy(
            src_ref=src, dst_ref=dst, send_sem=ssem.at[k], recv_sem=rsem.at[k],
            device_id=to, device_id_type=MESH,
        )
        c.start()
        started.append(c)
        return c

    def shift(axis, n, me, d):
        return {axis: lax.rem(me + d + n, n)}

    def ypeers():
        for dl in range(NYL):
            for dh in range(NYH):
                for dc in range(NCO):
                    if dl or dh or dc:
                        yield {
                            "ylo": lax.rem(yl + dl, NYL),
                            "yhi": lax.rem(yh + dh, NYH),
                            "core": lax.rem(co + dc, NCO),
                        }

    partner = {"core": 1 - co}
    ypair = {"ylo": 1 - yl}

    local = [
        pltpu.make_async_copy(virt, VIRT.at[pl.ds(x * 1024, 1024)], lsem.at[0]),
        pltpu.make_async_copy(occ.at[pl.ds(a * 128, 128)], OCC.at[yl * 8 + z], lsem.at[1]),
        pltpu.make_async_copy(ints, AV, lsem.at[2]),
    ]
    for c in local:
        c.start()

    barrier = pltpu.get_barrier_semaphore()
    zx = [
        {"row": lax.rem(x + dx, NX), "z": lax.rem(z + dz, NZ)}
        for dx in range(NX) for dz in range(NZ) if dx or dz
    ]
    diag = [{"ylo": 1 - yl, "z": lax.rem(z + d + NZ, NZ)} for d in (1, -1)]
    peers = zx + diag + list(ypeers())
    for p in peers:
        pl.semaphore_signal(barrier, inc=1, device_id=p, device_id_type=MESH)
    pl.semaphore_wait(barrier, len(peers))

    def vq(r, half, quarter):
        return VIRT.at[pl.ds(r * 1024 + half * 512 + quarter * 256, 256)]

    def own_vq(quarter):
        return virt.at[pl.ds(co * 512 + quarter * 256, 256)]

    def xblk(d):
        return lax.rem(x + d + NX, NX)

    def occ_half(c, h):
        return OCC.at[c, pl.ds(h * 64, 64)]

    def own_half(h):
        return occ.at[pl.ds(a * 128 + h * 64, 64)]

    def zat(d):
        return lax.rem(z + d + NZ, NZ)

    SIGN = {"+": 1, "-": -1}
    xs = {}
    for d, order in (("+", (0, 1)), ("-", (1, 0))):
        xs[d] = [
            send(own_vq(q), vq(x, co, q), **shift("row", NX, x, SIGN[d])) for q in order
        ]
    cme = yl * 8 + z
    base = {"O": yl * 8, "P": (1 - yl) * 8}
    order = {"+": (0, 1), "-": (1, 0)}
    zs = {}
    zy = []
    for k in range(2):
        for L in "OP":
            for d in "+-":
                h = order[d][k]
                to = shift("z", NZ, z, SIGN[d])
                if L == "P":
                    to["ylo"] = 1 - yl
                zs[L, d, 1, h] = send(own_half(h), occ_half(cme, h), **to)
        zy.append(send(own_half(k), occ_half(cme, k), **ypair))

    lane = iota((8, 128), 1)
    subl = iota((8, 128), 0)
    idx = [listed[0, n] for n in range(8)]
    own = [lax.shift_right_logical(v, 3) for v in idx]
    pos = [jnp.bitwise_and(v, 7) for v in idx]
    rank = []
    for n in range(8):
        r = jnp.int32(0)
        for m in range(n):
            r = r + jnp.where(own[m] == own[n], 1, 0).astype(jnp.int32)
        rank.append(r)
    table = jnp.zeros((8, 128), F32)
    for n in range(8):
        hit = (subl == own[n]) & (lane // 4 == a * 2 + rank[n])
        table = table + jnp.where(hit, (pos[n] + 1).astype(F32), 0.0)
    LSRC[...] = table
    LB[a] = table
    lab = []
    for dh in range(NYH):
        for dc in range(NCO):
            if dh or dc:
                lab.append(
                    send(LSRC, LB.at[a], yhi=lax.rem(yh + dh, NYH), core=lax.rem(co + dc, NCO))
                )

    def relay(step):
        for k in range(2):
            for L in "OP":
                for d in "+-":
                    s = SIGN[d]
                    h = order[d][k]
                    zs[L, d, step, h].wait_recv()
                    blk = occ_half(base[L] + zat(-s * step), h)
                    if step <= 2:
                        zs[L, d, step + 1, h] = send(blk, blk, **shift("z", NZ, z, s))
                    if step == 2 and k == 0:
                        zs[L, d, 4, h] = send(blk, blk, **shift("z", NZ, z, 2 * s))

    fwd = []

    def xfwd(r, q):
        fwd.append(send(vq(r, co, q), vq(r, co, q), **partner))

    relay(1)
    for d, q in (("+", 0), ("-", 1)):
        s = SIGN[d]
        xs[d][0].wait_recv()
        r = xblk(-s)
        xs[d].append(send(vq(r, co, q), vq(r, co, q), **shift("row", NX, x, s)))
        xfwd(r, q)
    relay(2)
    for d, q in (("+", 1), ("-", 0)):
        xs[d][1].wait_recv()
        xfwd(xblk(-SIGN[d]), q)
    for d, q in (("+", 0), ("-", 1)):
        xs[d][2].wait_recv()
        xfwd(xblk(2), q)
    for c in local[:2]:
        c.wait()
    for c in zy:
        c.wait_recv()
    for c in lab:
        c.wait_recv()
    for c in fwd:
        c.wait_recv()

    def mm(c, acc):
        return acc + jnp.dot(
            OCC[c], VIRT[pl.ds(pl.multiple_of(c * 256, 256), 256), :], preferred_element_type=F32
        )

    acc = jnp.zeros((128, 256), F32)
    for dist in (0, 1, -1, 2, -2):
        for L in "OP":
            acc = mm(base[L] + zat(dist), acc)
    relay(3)
    for dist in (3, -3):
        for L in "OP":
            acc = mm(base[L] + zat(dist), acc)
    for L in "OP":
        for d in "+-":
            zs[L, d, 4, order[d][0]].wait_recv()
        acc = mm(base[L] + zat(4), acc)
    PR[...] = acc.astype(BF)
    for q in range(2):
        ROWS[q] = acc[:, q * 128 : (q + 1) * 128]
    tiles_from_rows(ROWS, FL)
    for m in range(32):
        BV[:, m * 128 : (m + 1) * 128] = FL[m * 8 : (m + 1) * 8, :]

    labels = LB[0]
    for o in range(1, 8):
        labels = labels + LB[o]
    labels = jnp.sum(jnp.where(subl == a, labels, 0.0), axis=0, keepdims=True)[:, 0:64]
    square = jnp.broadcast_to(labels, (64, 64))
    labels_down = jnp.sum(
        jnp.where(iota((64, 64), 0) == iota((64, 64), 1), square, 0.0), axis=1, keepdims=True
    )
    i64 = iota((64, 8), 0)
    n8 = iota((64, 8), 1)
    q64 = jnp.bitwise_and(i64, 3)
    out = jnp.zeros((64, 1024), F32)
    for q in range(4):
        take = jnp.where((labels_down == (n8 + 1).astype(F32)) & (q64 == q), 1.0, 0.0)
        out = out + jnp.dot(
            take.astype(BF), BV[:, q * 1024 : (q + 1) * 1024].astype(BF), preferred_element_type=F32
        )
    for o in range(8):
        ST[o] = out[o * 8 : (o + 1) * 8, :].astype(BF)

    def to_owners(src, dst, sem):
        keep = pltpu.make_async_copy(src.at[a], dst.at[a], sem)
        keep.start()
        cs = []
        for dh in (2, 1, 3, 0):
            for dc in range(NCO):
                if dh or dc:
                    h2 = lax.rem(yh + dh, NYH)
                    c2 = lax.rem(co + dc, NCO)
                    cs.append(send(src.at[h2 * 2 + c2], dst.at[a], yhi=h2, core=c2))
        return keep, cs

    keep, cs = to_owners(ST, RT, lsem.at[3])
    keep.wait()
    for c in cs:
        c.wait_recv()

    def prow(o):
        return prod_out.at[pl.ds(o * 128, 128)]

    pown = pltpu.make_async_copy(PR, prow(a), lsem.at[4])
    pown.start()
    pcore = send(PR, prow(a), **partner)
    pfar = [send(PR, prow(a), **shift("yhi", NYH, yh, d)) for d in (1, 3, 2)]

    arrived = jnp.concatenate([RT[o].astype(F32) for o in range(8)], axis=0).astype(BF)
    s64 = iota((8, 64), 1)
    n64 = iota((8, 64), 0)
    chosen = []
    for q in range(4):
        pick = jnp.zeros((8, 64), F32)
        for n in range(8):
            hit = (n64 == n) & (s64 == own[n] * 8 + rank[n] * 4 + q)
            pick = pick + jnp.where(hit, 1.0, 0.0)
        chosen.append(jnp.dot(pick.astype(BF), arrived, preferred_element_type=F32))
    chosen = jnp.concatenate(chosen, axis=1)
    local[2].wait()

    def contract(p, _):
        v = AV[p].astype(F32) * chosen
        s = v[:, 0:128]
        for m in range(1, 32):
            s = s + v[:, m * 128 : (m + 1) * 128]
        ACC[p] = s
        return 0

    lax.fori_loop(0, 32, contract, 0, unroll=2)
    part = jnp.sum(jnp.sum(ACC[...], axis=1), axis=1, keepdims=True)
    lane32 = iota((32, 128), 1)
    sub32 = iota((32, 128), 0)
    spread = jnp.where(lane32 == sub32 + lax.rem(a, 4) * 32, part, 0.0)
    spread = jnp.sum(spread, axis=0, keepdims=True)
    coeff = jnp.where(subl == a // 4, jnp.broadcast_to(spread, (8, 128)), 0.0)

    def exchange(k, value, buf, slot, targets, n):
        CSRC[k] = value
        buf[slot] = value
        cs = [send(CSRC.at[k], buf.at[slot], **t) for t in targets]
        for c in cs:
            c.wait_recv()
        total = buf[0]
        for i in range(1, n):
            total = total + buf[i]
        return total

    coeff = exchange(0, coeff, CZX, x * 8 + z, zx, NX * NZ)
    pfwd = []
    for c, d in zip(pfar, (1, 3, 2)):
        c.wait_recv()
        o = lax.rem(yh + NYH - d, NYH) * 2 + co
        pfwd.append(send(prow(o), prow(o), **partner))
    coeff = exchange(1, coeff, CY, yl * 8 + a, list(ypeers()), 16)

    row = jnp.sum(jnp.where(subl == a // 4, coeff, 0.0), axis=0, keepdims=True)
    mine = jnp.zeros((1, 32), F32)
    for k in range(4):
        mine = mine + jnp.where(lax.rem(a, 4) == k, row[:, k * 32 : (k + 1) * 32], 0.0)
    coeff_out[...] = mine

    scr = metric[:, 0:128] * coeff[0:1, :] + metric[:, 128:256] * coeff[1:2, :]
    scr = jnp.sum(scr, axis=1, keepdims=True)
    SCB[...] = jnp.broadcast_to(scr, (32, 128))

    def weigh(p, accs):
        s = SCB[pl.ds(p, 1), :]
        v = AV[p].astype(F32)
        return tuple(accs[m] + v[:, m * 128 : (m + 1) * 128] * s for m in range(32))

    accs = lax.fori_loop(
        0, 32, weigh, tuple(jnp.zeros((8, 128), F32) for _ in range(32))
    )
    for m in range(32):
        BV[:, m * 128 : (m + 1) * 128] = accs[m]
    out = jnp.zeros((64, 1024), F32)
    for q in range(4):
        sel = jnp.zeros((64, 8), F32)
        for n in range(8):
            hit = (n8 == n) & (i64 == own[n] * 8 + rank[n] * 4 + q)
            sel = sel + jnp.where(hit, 1.0, 0.0)
        out = out + jnp.dot(
            sel.astype(BF), BV[:, q * 1024 : (q + 1) * 1024].astype(BF), preferred_element_type=F32
        )
    for o in range(8):
        SB[o] = out[o * 8 : (o + 1) * 8, :].astype(BF)
    keep, cs = to_owners(SB, RB, lsem.at[3])
    t64 = iota((8, 64), 0).astype(F32)
    l64 = jnp.bitwise_and(iota((8, 64), 1), 3)
    keep.wait()
    for c in cs:
        c.wait_recv()
    arrived = jnp.concatenate([RB[o].astype(F32) for o in range(8)], axis=0).astype(BF)
    for q in range(4):
        place = jnp.where((labels == t64 + 1.0) & (l64 == q), 1.0, 0.0).astype(BF)
        d = jnp.dot(place, arrived, preferred_element_type=F32)
        for m in range(8):
            FL[(q * 8 + m) * 8 : (q * 8 + m + 1) * 8, :] = d[:, m * 128 : (m + 1) * 128]
    rows_from_tiles(FL, ROWS)
    deriv = jnp.concatenate([ROWS[0], ROWS[1]], axis=1).astype(BF)

    def partial(i):
        return lax.dot_general(
            VIRT[pl.ds(pl.multiple_of(i * 256, 256), 256), :], deriv,
            (((1,), (1,)), ((), ())), preferred_element_type=F32,
        )

    IL = {"O": 0, "P": 1}
    ID = {"+": 0, "-": 1}
    fs = {}
    for L in "OP":
        v = partial(base[L] + zat(4))
        for d in "+-":
            h = order[d][0]
            i, j = IL[L], ID[d]
            S4[i, j] = v[h * 128 : (h + 1) * 128].astype(BF)
            fs[L, d, 4] = send(S4.at[i, j], R4.at[i, j], **shift("z", NZ, z, 2 * SIGN[d]))
    for L in "OP":
        for d in "+-":
            i, j = IL[L], ID[d]
            v = partial(base[L] + zat(3 * SIGN[d]))
            for h in order[d]:
                S3[i, j, h] = v[h * 128 : (h + 1) * 128].astype(BF)
                fs[L, d, 3, h] = send(
                    S3.at[i, j, h], R3.at[i, j, h], **shift("z", NZ, z, SIGN[d])
                )
    for dist in (2, -2, 1, -1, 0):
        for L in "OP":
            FP[base[L] + zat(dist)] = partial(base[L] + zat(dist))
    fy = []
    for h in range(2):
        SY[h] = FP[base["P"] + z, h * 128 : (h + 1) * 128, :].astype(BF)
        fy.append(send(SY.at[h], RY.at[h], **ypair))

    for k in (1, 0):
        for L in "OP":
            for d in "+-":
                i, j, s = IL[L], ID[d], SIGN[d]
                h = order[d][k]
                v = FP[base[L] + zat(2 * s), h * 128 : (h + 1) * 128, :]
                fs[L, d, 3, h].wait_recv()
                v = v + R3[i, j, h].astype(F32)
                if k == 0:
                    fs[L, d, 4].wait_recv()
                    v = v + R4[i, j].astype(F32)
                S2[i, j, h] = v.astype(BF)
                fs[L, d, 2, h] = send(S2.at[i, j, h], R2.at[i, j, h], **shift("z", NZ, z, s))
    for k in (1, 0):
        for L in "OP":
            for d in "+-":
                i, j, s = IL[L], ID[d], SIGN[d]
                h = order[d][k]
                v = FP[base[L] + zat(s), h * 128 : (h + 1) * 128, :]
                fs[L, d, 2, h].wait_recv()
                v = v + R2[i, j, h].astype(F32)
                S1[i, j, h] = v.astype(BF)
                to = shift("z", NZ, z, s)
                if L == "P":
                    to["ylo"] = 1 - yl
                fs[L, d, 1, h] = send(S1.at[i, j, h], R1.at[i, j, h], **to)
    pown.wait()
    pcore.wait_recv()
    for c in pfwd:
        c.wait_recv()
    for h in range(2):
        fy[h].wait_recv()
        v = FP[base["O"] + z, h * 128 : (h + 1) * 128, :] + RY[h].astype(F32)
        for L in "OP":
            for d in "+-":
                fs[L, d, 1, h].wait_recv()
                v = v + R1[IL[L], ID[d], h].astype(F32)
        force_out[h * 128 : (h + 1) * 128, :] = v
    for c in started:
        c.wait_send()
    assert count[0] <= NCOPY


def on_device(green_occ, green_virt, integrals, listed, metric):
    vm = pltpu.VMEM
    hbm = pl.BlockSpec(memory_space=pl.ANY)
    inv = pl.BlockSpec(memory_space=pltpu.VMEM)
    product, coeff, force = pl.pallas_call(
        body,
        out_shape=(
            jax.ShapeDtypeStruct((1024, 256), BF),
            jax.ShapeDtypeStruct((1, 32), F32),
            jax.ShapeDtypeStruct((256, 128), F32),
        ),
        in_specs=[pl.BlockSpec(memory_space=pltpu.SMEM), hbm, hbm, hbm, inv],
        out_specs=(hbm, inv, inv),
        scratch_shapes=[
            vm((4096, 256), BF),
            vm((16, 128, 256), BF),
            vm((32, 8, 4096), BF),
            vm((256, 128), F32),
            vm((2, 128, 128), F32),
            vm((128, 256), BF),
            vm((2, 8, 128), F32),
            vm((32, 8, 128), F32),
            vm((16, 8, 128), F32),
            vm((32, 8, 128), F32),
            vm((32, 128), F32),
            vm((8, 128), F32),
            vm((8, 8, 128), F32),
            vm((8, 4096), F32),
            vm((8, 8, 1024), BF),
            vm((8, 8, 1024), BF),
            vm((8, 8, 1024), BF),
            vm((8, 8, 1024), BF),
            vm((16, 256, 128), F32),
            vm((2, 2, 128, 128), BF),
            vm((2, 2, 128, 128), BF),
            vm((2, 2, 2, 128, 128), BF),
            vm((2, 2, 2, 128, 128), BF),
            vm((2, 2, 2, 128, 128), BF),
            vm((2, 2, 2, 128, 128), BF),
            vm((2, 2, 2, 128, 128), BF),
            vm((2, 2, 2, 128, 128), BF),
            vm((2, 128, 128), BF),
            vm((2, 128, 128), BF),
            pltpu.SemaphoreType.DMA((NCOPY,)),
            pltpu.SemaphoreType.DMA((NCOPY,)),
            pltpu.SemaphoreType.DMA((5,)),
        ],
        compiler_params=pltpu.CompilerParams(
            collective_id=0, has_side_effects=True, vmem_limit_bytes=60 << 20
        ),
        name="force_window",
    )(
        listed.reshape(1, 8), green_occ, green_virt, integrals.reshape(32, 8, 4096), metric
    )
    return product, coeff.reshape(32), force


def solution(mesh):
    split = Mesh(
        mesh.devices.reshape(NX, NYL, NZ, NYH, NCO), ("row", "ylo", "z", "yhi", "core")
    )
    col, aux = ("ylo", "z"), ("yhi", "core")
    return jax.shard_map(
        on_device,
        mesh=split,
        in_specs=(
            P("row", col),
            P("row", col),
            P("row", col, aux, None, None),
            P("row", col, aux, None),
            P(aux, None),
        ),
        out_specs=(P("row", col), P(aux), P(col, ("row", *aux))),
        check_vma=False,
    )
```

```python
import jax
import jax.numpy as jnp
from jax import lax
from jax.experimental import pallas as pl
from jax.experimental.pallas import tpu as pltpu
from jax.sharding import Mesh
from jax.sharding import PartitionSpec as P

MESH = pl.DeviceIdType.MESH
BF = jnp.bfloat16
F32 = jnp.float32
NX, NYL, NZ, NYH, NCO = 4, 2, 8, 4, 2
NCOPY = 160


def iota(shape, dim):
    return lax.broadcasted_iota(jnp.int32, shape, dim)


def rows_from_tiles(fl, rows):
    left = iota((32, 128), 1) < 64
    for br in range(2):
        for q in range(2):
            t = br * 4 + 2 * q
            a = fl[pl.ds(t, 32, stride=8), :]
            b = fl[pl.ds(t + 1, 32, stride=8), :]
            even = jnp.where(left, a, pltpu.roll(b, 64, 1))
            odd = jnp.where(left, pltpu.roll(a, 64, 1), b)
            rows[q, pl.ds(br * 64, 32, stride=2), :] = even
            rows[q, pl.ds(br * 64 + 1, 32, stride=2), :] = odd


def tiles_from_rows(rows, fl):
    left = iota((32, 128), 1) < 64
    for br in range(2):
        for q in range(2):
            t = br * 4 + 2 * q
            even = rows[q, pl.ds(br * 64, 32, stride=2), :]
            odd = rows[q, pl.ds(br * 64 + 1, 32, stride=2), :]
            fl[pl.ds(t, 32, stride=8), :] = jnp.where(left, even, pltpu.roll(odd, 64, 1))
            fl[pl.ds(t + 1, 32, stride=8), :] = jnp.where(left, pltpu.roll(even, 64, 1), odd)


def body(
    listed, occ, virt, ints, metric, prod_out, coeff_out, force_out,
    VIRT, OCC, AV, FL, ROWS, PR, CSRC, CZX, CY, ACC, SCB, LSRC, LB,
    BV, SB, RB, ST, RT, FP, S4, R4, S3, R3, S2, R2, S1, R1, SY, RY, ssem, rsem, lsem,
):
    x = lax.axis_index("row")
    yl = lax.axis_index("ylo")
    z = lax.axis_index("z")
    yh = lax.axis_index("yhi")
    co = lax.axis_index("core")
    a = yh * 2 + co
    count = [0]
    started = []

    def send(src, dst, **to):
        k = count[0]
        count[0] += 1
        c = pltpu.make_async_remote_copy(
            src_ref=src, dst_ref=dst, send_sem=ssem.at[k], recv_sem=rsem.at[k],
            device_id=to, device_id_type=MESH,
        )
        c.start()
        started.append(c)
        return c

    def shift(axis, n, me, d):
        return {axis: lax.rem(me + d + n, n)}

    def ypeers():
        for dl in range(NYL):
            for dh in range(NYH):
                for dc in range(NCO):
                    if dl or dh or dc:
                        yield {
                            "ylo": lax.rem(yl + dl, NYL),
                            "yhi": lax.rem(yh + dh, NYH),
                            "core": lax.rem(co + dc, NCO),
                        }

    partner = {"core": 1 - co}
    ypair = {"ylo": 1 - yl}

    local = [
        pltpu.make_async_copy(virt, VIRT.at[pl.ds(x * 1024, 1024)], lsem.at[0]),
        pltpu.make_async_copy(occ.at[pl.ds(a * 128, 128)], OCC.at[yl * 8 + z], lsem.at[1]),
        pltpu.make_async_copy(ints, AV, lsem.at[2]),
    ]
    for c in local:
        c.start()

    barrier = pltpu.get_barrier_semaphore()
    zx = [
        {"row": lax.rem(x + dx, NX), "z": lax.rem(z + dz, NZ)}
        for dx in range(NX) for dz in range(NZ) if dx or dz
    ]
    diag = [{"ylo": 1 - yl, "z": lax.rem(z + d + NZ, NZ)} for d in (1, -1)]
    peers = zx + diag + list(ypeers())
    for p in peers:
        pl.semaphore_signal(barrier, inc=1, device_id=p, device_id_type=MESH)
    pl.semaphore_wait(barrier, len(peers))

    def vq(r, half, quarter):
        return VIRT.at[pl.ds(r * 1024 + half * 512 + quarter * 256, 256)]

    def own_vq(quarter):
        return virt.at[pl.ds(co * 512 + quarter * 256, 256)]

    def xblk(d):
        return lax.rem(x + d + NX, NX)

    def occ_half(c, h):
        return OCC.at[c, pl.ds(h * 64, 64)]

    def own_half(h):
        return occ.at[pl.ds(a * 128 + h * 64, 64)]

    def zat(d):
        return lax.rem(z + d + NZ, NZ)

    SIGN = {"+": 1, "-": -1}
    cme = yl * 8 + z
    base = {"O": yl * 8, "P": (1 - yl) * 8}
    order = {"+": (0, 1), "-": (1, 0)}
    zs = {}
    zy = []
    for k in range(2):
        for L in "PO":
            for d in "+-":
                h = order[d][k]
                to = shift("z", NZ, z, SIGN[d])
                if L == "P":
                    to["ylo"] = 1 - yl
                zs[L, d, 1, h] = send(own_half(h), occ_half(cme, h), **to)
    xs = {}
    for d, quarters in (("+", (0, 1)), ("-", (1, 0))):
        xs[d] = [
            send(own_vq(q), vq(x, co, q), **shift("row", NX, x, SIGN[d])) for q in quarters
        ]
    lane = iota((8, 128), 1)
    subl = iota((8, 128), 0)
    idx = [listed[0, n] for n in range(8)]
    own = [lax.shift_right_logical(v, 3) for v in idx]
    pos = [jnp.bitwise_and(v, 7) for v in idx]
    rank = []
    for n in range(8):
        r = jnp.int32(0)
        for m in range(n):
            r = r + jnp.where(own[m] == own[n], 1, 0).astype(jnp.int32)
        rank.append(r)
    table = jnp.zeros((8, 128), F32)
    for n in range(8):
        hit = (subl == own[n]) & (lane // 4 == a * 2 + rank[n])
        table = table + jnp.where(hit, (pos[n] + 1).astype(F32), 0.0)
    LSRC[...] = table
    LB[a] = table
    lab = []
    for dh in range(NYH):
        for dc in range(NCO):
            if dh or dc:
                lab.append(
                    send(LSRC, LB.at[a], yhi=lax.rem(yh + dh, NYH), core=lax.rem(co + dc, NCO))
                )

    for h in range(2):
        zy.append(send(own_half(h), occ_half(cme, h), **ypair))

    def relay(step):
        for k in range(2):
            for L in "OP":
                for d in "+-":
                    s = SIGN[d]
                    h = order[d][k]
                    zs[L, d, step, h].wait_recv()
                    blk = occ_half(base[L] + zat(-s * step), h)
                    if step <= 2:
                        zs[L, d, step + 1, h] = send(blk, blk, **shift("z", NZ, z, s))
                    if step == 2 and k == 0:
                        zs[L, d, 4, h] = send(blk, blk, **shift("z", NZ, z, 2 * s))

    fwd = []

    def xfwd(r, q):
        fwd.append(send(vq(r, co, q), vq(r, co, q), **partner))

    relay(1)
    for d, q in (("+", 0), ("-", 1)):
        s = SIGN[d]
        xs[d][0].wait_recv()
        r = xblk(-s)
        xs[d].append(send(vq(r, co, q), vq(r, co, q), **shift("row", NX, x, s)))
        xfwd(r, q)
    relay(2)
    for d, q in (("+", 1), ("-", 0)):
        xs[d][1].wait_recv()
        xfwd(xblk(-SIGN[d]), q)
    for d, q in (("+", 0), ("-", 1)):
        xs[d][2].wait_recv()
        xfwd(xblk(2), q)
    for c in local[:2]:
        c.wait()
    for c in zy:
        c.wait_recv()
    for c in lab:
        c.wait_recv()
    for c in fwd:
        c.wait_recv()

    def mm(c, acc):
        return acc + jnp.dot(
            OCC[c], VIRT[pl.ds(pl.multiple_of(c * 256, 256), 256), :], preferred_element_type=F32
        )

    acc = jnp.zeros((128, 256), F32)
    for dist in (0, 1, -1, 2, -2):
        for L in "OP":
            acc = mm(base[L] + zat(dist), acc)
    relay(3)
    for dist in (3, -3):
        for L in "OP":
            acc = mm(base[L] + zat(dist), acc)
    for L in "OP":
        for d in "+-":
            zs[L, d, 4, order[d][0]].wait_recv()
        acc = mm(base[L] + zat(4), acc)
    PR[...] = acc.astype(BF)
    for q in range(2):
        ROWS[q] = acc[:, q * 128 : (q + 1) * 128]
    tiles_from_rows(ROWS, FL)
    for m in range(32):
        BV[:, m * 128 : (m + 1) * 128] = FL[m * 8 : (m + 1) * 8, :]

    labels = LB[0]
    for o in range(1, 8):
        labels = labels + LB[o]
    labels = jnp.sum(jnp.where(subl == a, labels, 0.0), axis=0, keepdims=True)[:, 0:64]
    square = jnp.broadcast_to(labels, (64, 64))
    labels_down = jnp.sum(
        jnp.where(iota((64, 64), 0) == iota((64, 64), 1), square, 0.0), axis=1, keepdims=True
    )
    i64 = iota((64, 8), 0)
    n8 = iota((64, 8), 1)
    q64 = jnp.bitwise_and(i64, 3)
    out = jnp.zeros((64, 1024), F32)
    for q in range(4):
        take = jnp.where((labels_down == (n8 + 1).astype(F32)) & (q64 == q), 1.0, 0.0)
        out = out + jnp.dot(
            take.astype(BF), BV[:, q * 1024 : (q + 1) * 1024].astype(BF), preferred_element_type=F32
        )
    for o in range(8):
        ST[o] = out[o * 8 : (o + 1) * 8, :].astype(BF)

    def to_owners(src, dst, sem):
        keep = pltpu.make_async_copy(src.at[a], dst.at[a], sem)
        keep.start()
        cs = []
        for dh in (2, 1, 3, 0):
            for dc in range(NCO):
                if dh or dc:
                    h2 = lax.rem(yh + dh, NYH)
                    c2 = lax.rem(co + dc, NCO)
                    cs.append(send(src.at[h2 * 2 + c2], dst.at[a], yhi=h2, core=c2))
        return keep, cs

    keep, cs = to_owners(ST, RT, lsem.at[3])
    keep.wait()
    for c in cs:
        c.wait_recv()

    def prow(o):
        return prod_out.at[pl.ds(o * 128, 128)]

    pown = pltpu.make_async_copy(PR, prow(a), lsem.at[4])
    pown.start()
    pcore = send(PR, prow(a), **partner)
    pfar = [send(PR, prow(a), **shift("yhi", NYH, yh, d)) for d in (1, 3, 2)]

    arrived = jnp.concatenate([RT[o].astype(F32) for o in range(8)], axis=0).astype(BF)
    s64 = iota((8, 64), 1)
    n64 = iota((8, 64), 0)
    chosen = []
    for q in range(4):
        pick = jnp.zeros((8, 64), F32)
        for n in range(8):
            hit = (n64 == n) & (s64 == own[n] * 8 + rank[n] * 4 + q)
            pick = pick + jnp.where(hit, 1.0, 0.0)
        chosen.append(jnp.dot(pick.astype(BF), arrived, preferred_element_type=F32))
    chosen = jnp.concatenate(chosen, axis=1)
    local[2].wait()

    def contract(p, _):
        v = AV[p].astype(F32) * chosen
        s = v[:, 0:128]
        for m in range(1, 32):
            s = s + v[:, m * 128 : (m + 1) * 128]
        ACC[p] = s
        return 0

    lax.fori_loop(0, 32, contract, 0, unroll=2)
    part = jnp.sum(jnp.sum(ACC[...], axis=1), axis=1, keepdims=True)
    lane32 = iota((32, 128), 1)
    sub32 = iota((32, 128), 0)
    spread = jnp.where(lane32 == sub32 + lax.rem(a, 4) * 32, part, 0.0)
    spread = jnp.sum(spread, axis=0, keepdims=True)
    coeff = jnp.where(subl == a // 4, jnp.broadcast_to(spread, (8, 128)), 0.0)

    def exchange(k, value, buf, slot, targets, n):
        CSRC[k] = value
        buf[slot] = value
        cs = [send(CSRC.at[k], buf.at[slot], **t) for t in targets]
        for c in cs:
            c.wait_recv()
        total = buf[0]
        for i in range(1, n):
            total = total + buf[i]
        return total

    coeff = exchange(0, coeff, CZX, x * 8 + z, zx, NX * NZ)
    pfwd = []
    for c, d in zip(pfar, (1, 3, 2)):
        c.wait_recv()
        o = lax.rem(yh + NYH - d, NYH) * 2 + co
        pfwd.append(send(prow(o), prow(o), **partner))
    coeff = exchange(1, coeff, CY, yl * 8 + a, list(ypeers()), 16)

    row = jnp.sum(jnp.where(subl == a // 4, coeff, 0.0), axis=0, keepdims=True)
    mine = jnp.zeros((1, 32), F32)
    for k in range(4):
        mine = mine + jnp.where(lax.rem(a, 4) == k, row[:, k * 32 : (k + 1) * 32], 0.0)
    coeff_out[...] = mine

    scr = metric[:, 0:128] * coeff[0:1, :] + metric[:, 128:256] * coeff[1:2, :]
    scr = jnp.sum(scr, axis=1, keepdims=True)
    SCB[...] = jnp.broadcast_to(scr, (32, 128))

    def weigh(p, accs):
        s = SCB[pl.ds(p, 1), :]
        v = AV[p].astype(F32)
        return tuple(accs[m] + v[:, m * 128 : (m + 1) * 128] * s for m in range(32))

    accs = lax.fori_loop(
        0, 32, weigh, tuple(jnp.zeros((8, 128), F32) for _ in range(32))
    )
    for m in range(32):
        BV[:, m * 128 : (m + 1) * 128] = accs[m]
    out = jnp.zeros((64, 1024), F32)
    for q in range(4):
        sel = jnp.zeros((64, 8), F32)
        for n in range(8):
            hit = (n8 == n) & (i64 == own[n] * 8 + rank[n] * 4 + q)
            sel = sel + jnp.where(hit, 1.0, 0.0)
        out = out + jnp.dot(
            sel.astype(BF), BV[:, q * 1024 : (q + 1) * 1024].astype(BF), preferred_element_type=F32
        )
    for o in range(8):
        SB[o] = out[o * 8 : (o + 1) * 8, :].astype(BF)
    keep, cs = to_owners(SB, RB, lsem.at[3])
    t64 = iota((8, 64), 0).astype(F32)
    l64 = jnp.bitwise_and(iota((8, 64), 1), 3)
    keep.wait()
    for c in cs:
        c.wait_recv()
    arrived = jnp.concatenate([RB[o].astype(F32) for o in range(8)], axis=0).astype(BF)
    for q in range(4):
        place = jnp.where((labels == t64 + 1.0) & (l64 == q), 1.0, 0.0).astype(BF)
        d = jnp.dot(place, arrived, preferred_element_type=F32)
        for m in range(8):
            FL[(q * 8 + m) * 8 : (q * 8 + m + 1) * 8, :] = d[:, m * 128 : (m + 1) * 128]
    rows_from_tiles(FL, ROWS)
    deriv = jnp.concatenate([ROWS[0], ROWS[1]], axis=1).astype(BF)

    def partial(i):
        return lax.dot_general(
            VIRT[pl.ds(pl.multiple_of(i * 256, 256), 256), :], deriv,
            (((1,), (1,)), ((), ())), preferred_element_type=F32,
        )

    IL = {"O": 0, "P": 1}
    ID = {"+": 0, "-": 1}
    fs = {}
    def send3(L, d, h):
        i, j = IL[L], ID[d]
        fs[L, d, 3, h] = send(S3.at[i, j, h], R3.at[i, j, h], **shift("z", NZ, z, SIGN[d]))

    for L in "PO":
        for d in "+-":
            v = partial(base[L] + zat(3 * SIGN[d]))
            for h in range(2):
                S3[IL[L], ID[d], h] = v[h * 128 : (h + 1) * 128].astype(BF)
            send3(L, d, order[d][1])
    for L in "PO":
        v = partial(base[L] + zat(4))
        for d in "+-":
            h = order[d][0]
            i, j = IL[L], ID[d]
            S4[i, j] = v[h * 128 : (h + 1) * 128].astype(BF)
            fs[L, d, 4] = send(S4.at[i, j], R4.at[i, j], **shift("z", NZ, z, 2 * SIGN[d]))
    for L in "PO":
        for d in "+-":
            send3(L, d, order[d][0])
    for dist in (2, -2, 1, -1, 0):
        for L in "OP":
            FP[base[L] + zat(dist)] = partial(base[L] + zat(dist))
    fy = []
    for h in range(2):
        SY[h] = FP[base["P"] + z, h * 128 : (h + 1) * 128, :].astype(BF)
        fy.append(send(SY.at[h], RY.at[h], **ypair))

    for k in (1, 0):
        for L in "PO":
            for d in "+-":
                i, j, s = IL[L], ID[d], SIGN[d]
                h = order[d][k]
                v = FP[base[L] + zat(2 * s), h * 128 : (h + 1) * 128, :]
                fs[L, d, 3, h].wait_recv()
                v = v + R3[i, j, h].astype(F32)
                if k == 0:
                    fs[L, d, 4].wait_recv()
                    v = v + R4[i, j].astype(F32)
                S2[i, j, h] = v.astype(BF)
                fs[L, d, 2, h] = send(S2.at[i, j, h], R2.at[i, j, h], **shift("z", NZ, z, s))
    for k in (1, 0):
        for L in "PO":
            for d in "+-":
                i, j, s = IL[L], ID[d], SIGN[d]
                h = order[d][k]
                v = FP[base[L] + zat(s), h * 128 : (h + 1) * 128, :]
                fs[L, d, 2, h].wait_recv()
                v = v + R2[i, j, h].astype(F32)
                S1[i, j, h] = v.astype(BF)
                to = shift("z", NZ, z, s)
                if L == "P":
                    to["ylo"] = 1 - yl
                fs[L, d, 1, h] = send(S1.at[i, j, h], R1.at[i, j, h], **to)
    pown.wait()
    pcore.wait_recv()
    for c in pfwd:
        c.wait_recv()
    for h in range(2):
        fy[h].wait_recv()
        v = FP[base["O"] + z, h * 128 : (h + 1) * 128, :] + RY[h].astype(F32)
        for L in "OP":
            for d in "+-":
                fs[L, d, 1, h].wait_recv()
                v = v + R1[IL[L], ID[d], h].astype(F32)
        force_out[h * 128 : (h + 1) * 128, :] = v
    for c in started:
        c.wait_send()
    assert count[0] <= NCOPY


def on_device(green_occ, green_virt, integrals, listed, metric):
    vm = pltpu.VMEM
    hbm = pl.BlockSpec(memory_space=pl.ANY)
    inv = pl.BlockSpec(memory_space=pltpu.VMEM)
    product, coeff, force = pl.pallas_call(
        body,
        out_shape=(
            jax.ShapeDtypeStruct((1024, 256), BF),
            jax.ShapeDtypeStruct((1, 32), F32),
            jax.ShapeDtypeStruct((256, 128), F32),
        ),
        in_specs=[pl.BlockSpec(memory_space=pltpu.SMEM), hbm, hbm, hbm, inv],
        out_specs=(hbm, inv, inv),
        scratch_shapes=[
            vm((4096, 256), BF),
            vm((16, 128, 256), BF),
            vm((32, 8, 4096), BF),
            vm((256, 128), F32),
            vm((2, 128, 128), F32),
            vm((128, 256), BF),
            vm((2, 8, 128), F32),
            vm((32, 8, 128), F32),
            vm((16, 8, 128), F32),
            vm((32, 8, 128), F32),
            vm((32, 128), F32),
            vm((8, 128), F32),
            vm((8, 8, 128), F32),
            vm((8, 4096), F32),
            vm((8, 8, 1024), BF),
            vm((8, 8, 1024), BF),
            vm((8, 8, 1024), BF),
            vm((8, 8, 1024), BF),
            vm((16, 256, 128), F32),
            vm((2, 2, 128, 128), BF),
            vm((2, 2, 128, 128), BF),
            vm((2, 2, 2, 128, 128), BF),
            vm((2, 2, 2, 128, 128), BF),
            vm((2, 2, 2, 128, 128), BF),
            vm((2, 2, 2, 128, 128), BF),
            vm((2, 2, 2, 128, 128), BF),
            vm((2, 2, 2, 128, 128), BF),
            vm((2, 128, 128), BF),
            vm((2, 128, 128), BF),
            pltpu.SemaphoreType.DMA((NCOPY,)),
            pltpu.SemaphoreType.DMA((NCOPY,)),
            pltpu.SemaphoreType.DMA((5,)),
        ],
        compiler_params=pltpu.CompilerParams(
            collective_id=0, has_side_effects=True, vmem_limit_bytes=60 << 20
        ),
        name="force_window",
    )(
        listed.reshape(1, 8), green_occ, green_virt, integrals.reshape(32, 8, 4096), metric
    )
    return product, coeff.reshape(32), force


def solution(mesh):
    split = Mesh(
        mesh.devices.reshape(NX, NYL, NZ, NYH, NCO), ("row", "ylo", "z", "yhi", "core")
    )
    col, aux = ("ylo", "z"), ("yhi", "core")
    return jax.shard_map(
        on_device,
        mesh=split,
        in_specs=(
            P("row", col),
            P("row", col),
            P("row", col, aux, None, None),
            P("row", col, aux, None),
            P(aux, None),
        ),
        out_specs=(P("row", col), P(aux), P(col, ("row", *aux))),
        check_vma=False,
    )
```

```python
import jax
import jax.numpy as jnp
from jax import lax
from jax.experimental import pallas as pl
from jax.experimental.pallas import tpu as pltpu
from jax.sharding import Mesh
from jax.sharding import PartitionSpec as P

MESH = pl.DeviceIdType.MESH
BF = jnp.bfloat16
F32 = jnp.float32
NX, NYL, NZ, NYH, NCO = 4, 2, 8, 4, 2
NCOPY = 208


def iota(shape, dim):
    return lax.broadcasted_iota(jnp.int32, shape, dim)


def rows_from_tiles(fl, rows):
    left = iota((32, 128), 1) < 64
    for br in range(2):
        for q in range(2):
            t = br * 4 + 2 * q
            a = fl[pl.ds(t, 32, stride=8), :]
            b = fl[pl.ds(t + 1, 32, stride=8), :]
            even = jnp.where(left, a, pltpu.roll(b, 64, 1))
            odd = jnp.where(left, pltpu.roll(a, 64, 1), b)
            rows[q, pl.ds(br * 64, 32, stride=2), :] = even
            rows[q, pl.ds(br * 64 + 1, 32, stride=2), :] = odd


def tiles_from_rows(rows, fl):
    left = iota((32, 128), 1) < 64
    for br in range(2):
        for q in range(2):
            t = br * 4 + 2 * q
            even = rows[q, pl.ds(br * 64, 32, stride=2), :]
            odd = rows[q, pl.ds(br * 64 + 1, 32, stride=2), :]
            fl[pl.ds(t, 32, stride=8), :] = jnp.where(left, even, pltpu.roll(odd, 64, 1))
            fl[pl.ds(t + 1, 32, stride=8), :] = jnp.where(left, pltpu.roll(even, 64, 1), odd)


def body(
    listed, occ, virt, ints, metric, prod_out, coeff_out, force_out,
    VIRT, OCC, AV, FL, ROWS, PR, CSRC, CZX, CY, ACC, SCB, LSRC, LB,
    BV, SB, RB, ST, RT, FP, SS, RR, SY, RY, ssem, rsem, lsem, ready,
):
    x = lax.axis_index("row")
    yl = lax.axis_index("ylo")
    z = lax.axis_index("z")
    yh = lax.axis_index("yhi")
    co = lax.axis_index("core")
    a = yh * 2 + co
    count = [0]
    started = []

    def send(src, dst, **to):
        k = count[0]
        count[0] += 1
        c = pltpu.make_async_remote_copy(
            src_ref=src, dst_ref=dst, send_sem=ssem.at[k], recv_sem=rsem.at[k],
            device_id=to, device_id_type=MESH,
        )
        c.start()
        started.append(c)
        return c

    def shift(axis, n, me, d):
        return {axis: lax.rem(me + d + n, n)}

    def ypeers():
        for dl in range(NYL):
            for dh in range(NYH):
                for dc in range(NCO):
                    if dl or dh or dc:
                        yield {
                            "ylo": lax.rem(yl + dl, NYL),
                            "yhi": lax.rem(yh + dh, NYH),
                            "core": lax.rem(co + dc, NCO),
                        }

    partner = {"core": 1 - co}
    ypair = {"ylo": 1 - yl}

    local = [
        pltpu.make_async_copy(virt, VIRT.at[pl.ds(x * 1024, 1024)], lsem.at[0]),
        pltpu.make_async_copy(occ.at[pl.ds(a * 128, 128)], OCC.at[yl * 8 + z], lsem.at[1]),
        pltpu.make_async_copy(ints, AV, lsem.at[2]),
    ]
    for c in local:
        c.start()

    barrier = pltpu.get_barrier_semaphore()
    zx = [
        {"row": lax.rem(x + dx, NX), "z": lax.rem(z + dz, NZ)}
        for dx in range(NX) for dz in range(NZ) if dx or dz
    ]
    diag = [{"ylo": 1 - yl, "z": lax.rem(z + d + NZ, NZ)} for d in (1, -1)]
    peers = [shift("row", NX, x, d) for d in (1, -1)]
    peers += [shift("z", NZ, z, d) for d in (1, -1, 2, -2)]
    peers += diag + [ypair]
    peers += [
        {"yhi": lax.rem(yh + dh, NYH), "core": lax.rem(co + dc, NCO)}
        for dh in range(NYH) for dc in range(NCO) if dh or dc
    ]
    for p in peers:
        pl.semaphore_signal(barrier, inc=1, device_id=p, device_id_type=MESH)
    pl.semaphore_wait(barrier, len(peers))

    def vq(r, half, quarter):
        return VIRT.at[pl.ds(r * 1024 + half * 512 + quarter * 256, 256)]

    def own_vq(quarter):
        return virt.at[pl.ds(co * 512 + quarter * 256, 256)]

    def xblk(d):
        return lax.rem(x + d + NX, NX)

    def occ_half(c, h):
        return OCC.at[c, pl.ds(h * 64, 64)]

    def own_half(h):
        return occ.at[pl.ds(a * 128 + h * 64, 64)]

    def zat(d):
        return lax.rem(z + d + NZ, NZ)

    SIGN = {"+": 1, "-": -1}
    cme = yl * 8 + z
    base = {"O": yl * 8, "P": (1 - yl) * 8}
    order = {"+": (0, 1), "-": (1, 0)}
    zs = {}
    zy = []
    for k in range(2):
        for L in "PO":
            for d in "+-":
                h = order[d][k]
                to = shift("z", NZ, z, SIGN[d])
                if L == "P":
                    to["ylo"] = 1 - yl
                zs[L, d, 1, h] = send(own_half(h), occ_half(cme, h), **to)
    xs = {}
    for d, quarters in (("+", (0, 1)), ("-", (1, 0))):
        xs[d] = [
            send(own_vq(q), vq(x, co, q), **shift("row", NX, x, SIGN[d])) for q in quarters
        ]
    lane = iota((8, 128), 1)
    subl = iota((8, 128), 0)
    idx = [listed[0, n] for n in range(8)]
    own = [lax.shift_right_logical(v, 3) for v in idx]
    pos = [jnp.bitwise_and(v, 7) for v in idx]
    rank = []
    for n in range(8):
        r = jnp.int32(0)
        for m in range(n):
            r = r + jnp.where(own[m] == own[n], 1, 0).astype(jnp.int32)
        rank.append(r)
    table = jnp.zeros((8, 128), F32)
    for n in range(8):
        hit = (subl == own[n]) & (lane // 4 == a * 2 + rank[n])
        table = table + jnp.where(hit, (pos[n] + 1).astype(F32), 0.0)
    for o in range(8):
        LSRC[o] = table[o : o + 1, :]
    LB[a] = LSRC[a]
    lab = []
    for dh in range(NYH):
        for dc in range(NCO):
            if dh or dc:
                h2 = lax.rem(yh + dh, NYH)
                c2 = lax.rem(co + dc, NCO)
                lab.append(send(LSRC.at[h2 * 2 + c2], LB.at[a], yhi=h2, core=c2))

    for h in range(2):
        zy.append(send(own_half(h), occ_half(cme, h), **ypair))

    def relay(step):
        for k in range(2):
            for L in "OP":
                for d in "+-":
                    s = SIGN[d]
                    h = order[d][k]
                    zs[L, d, step, h].wait_recv()
                    blk = occ_half(base[L] + zat(-s * step), h)
                    if step <= 2:
                        zs[L, d, step + 1, h] = send(blk, blk, **shift("z", NZ, z, s))
                    if step == 2 and k == 0:
                        zs[L, d, 4, h] = send(blk, blk, **shift("z", NZ, z, 2 * s))

    fwd = []

    def xfwd(r, q):
        fwd.append(send(vq(r, co, q), vq(r, co, q), **partner))

    relay(1)
    for d, q in (("+", 0), ("-", 1)):
        s = SIGN[d]
        xs[d][0].wait_recv()
        r = xblk(-s)
        xs[d].append(send(vq(r, co, q), vq(r, co, q), **shift("row", NX, x, s)))
        xfwd(r, q)
    relay(2)
    for d, q in (("+", 1), ("-", 0)):
        xs[d][1].wait_recv()
        xfwd(xblk(-SIGN[d]), q)
    for d, q in (("+", 0), ("-", 1)):
        xs[d][2].wait_recv()
        xfwd(xblk(2), q)
    for c in local[:2]:
        c.wait()
    for c in zy:
        c.wait_recv()
    for c in lab:
        c.wait_recv()
    for c in fwd:
        c.wait_recv()

    def mm(c, acc):
        return acc + jnp.dot(
            OCC[c], VIRT[pl.ds(pl.multiple_of(c * 256, 256), 256), :], preferred_element_type=F32
        )

    acc = jnp.zeros((128, 256), F32)
    for dist in (0, 1, -1, 2, -2):
        for L in "OP":
            acc = mm(base[L] + zat(dist), acc)
    relay(3)
    for dist in (3, -3):
        for L in "OP":
            acc = mm(base[L] + zat(dist), acc)
    for L in "OP":
        for d in "+-":
            zs[L, d, 4, order[d][0]].wait_recv()
        acc = mm(base[L] + zat(4), acc)
    for d in range(1, NX):
        pl.semaphore_signal(
            ready, inc=1, device_id=shift("row", NX, x, d), device_id_type=MESH
        )
    PR[...] = acc.astype(BF)
    for q in range(2):
        ROWS[q] = acc[:, q * 128 : (q + 1) * 128]
    tiles_from_rows(ROWS, FL)
    for m in range(32):
        BV[:, m * 128 : (m + 1) * 128] = FL[m * 8 : (m + 1) * 8, :]

    labels = LB[0]
    for o in range(1, 8):
        labels = labels + LB[o]
    labels = labels[:, 0:64]
    square = jnp.broadcast_to(labels, (64, 64))
    labels_down = jnp.sum(
        jnp.where(iota((64, 64), 0) == iota((64, 64), 1), square, 0.0), axis=1, keepdims=True
    )
    i64 = iota((64, 8), 0)
    n8 = iota((64, 8), 1)
    q64 = jnp.bitwise_and(i64, 3)
    out = jnp.zeros((64, 1024), F32)
    for q in range(4):
        take = jnp.where((labels_down == (n8 + 1).astype(F32)) & (q64 == q), 1.0, 0.0)
        out = out + jnp.dot(
            take.astype(BF), BV[:, q * 1024 : (q + 1) * 1024].astype(BF), preferred_element_type=F32
        )
    for o in range(8):
        ST[o] = out[o * 8 : (o + 1) * 8, :].astype(BF)

    def to_owners(src, dst, sem):
        keep = pltpu.make_async_copy(src.at[a], dst.at[a], sem)
        keep.start()
        cs = []
        for dh in (2, 1, 3, 0):
            for dc in range(NCO):
                if dh or dc:
                    h2 = lax.rem(yh + dh, NYH)
                    c2 = lax.rem(co + dc, NCO)
                    cs.append(send(src.at[h2 * 2 + c2], dst.at[a], yhi=h2, core=c2))
        return keep, cs

    keep, cs = to_owners(ST, RT, lsem.at[3])
    keep.wait()
    for c in cs:
        c.wait_recv()

    def prow(o):
        return prod_out.at[pl.ds(o * 128, 128)]

    pown = pltpu.make_async_copy(PR, prow(a), lsem.at[4])
    pown.start()
    pcore = send(PR, prow(a), **partner)
    pfar = [send(PR, prow(a), **shift("yhi", NYH, yh, d)) for d in (1, 3, 2)]

    arrived = jnp.concatenate([RT[o].astype(F32) for o in range(8)], axis=0).astype(BF)
    s64 = iota((8, 64), 1)
    n64 = iota((8, 64), 0)
    chosen = []
    for q in range(4):
        pick = jnp.zeros((8, 64), F32)
        for n in range(8):
            hit = (n64 == n) & (s64 == own[n] * 8 + rank[n] * 4 + q)
            pick = pick + jnp.where(hit, 1.0, 0.0)
        chosen.append(jnp.dot(pick.astype(BF), arrived, preferred_element_type=F32))
    chosen = jnp.concatenate(chosen, axis=1)
    local[2].wait()

    def contract(p, _):
        v = AV[p].astype(F32) * chosen
        s = v[:, 0:128]
        for m in range(1, 32):
            s = s + v[:, m * 128 : (m + 1) * 128]
        ACC[p] = s
        return 0

    lax.fori_loop(0, 32, contract, 0, unroll=2)
    part = jnp.sum(jnp.sum(ACC[...], axis=1), axis=1, keepdims=True)
    lane32 = iota((32, 128), 1)
    sub32 = iota((32, 128), 0)
    spread = jnp.where(lane32 == sub32 + lax.rem(a, 4) * 32, part, 0.0)
    spread = jnp.sum(spread, axis=0, keepdims=True)

    def exchange(k, value, buf, slot, targets):
        CSRC[k] = value
        buf[slot] = value
        for c in [send(CSRC.at[k], buf.at[slot], **t) for t in targets]:
            c.wait_recv()

    pl.semaphore_wait(ready, NX - 1)
    exchange(0, spread, CZX, x * 8 + z, zx)
    total = CZX[0]
    for i in range(1, NX * NZ):
        total = total + CZX[i]
    exchange(1, total, CY, yl * 8 + a, list(ypeers()))
    halves = []
    for first in (0, 4):
        total = CY[first]
        for i in (1, 2, 3, 8, 9, 10, 11):
            total = total + CY[first + i]
        halves.append(total)

    row = jnp.where(a // 4 == 0, halves[0], halves[1])
    mine = jnp.zeros((1, 32), F32)
    for k in range(4):
        mine = mine + jnp.where(lax.rem(a, 4) == k, row[:, k * 32 : (k + 1) * 32], 0.0)
    coeff_out[...] = mine

    scr = metric[:, 0:128] * halves[0] + metric[:, 128:256] * halves[1]
    scr = jnp.sum(scr, axis=1, keepdims=True)
    SCB[...] = jnp.broadcast_to(scr, (32, 128))

    def weigh(p, accs):
        s = SCB[pl.ds(p, 1), :]
        v = AV[p].astype(F32)
        return tuple(accs[m] + v[:, m * 128 : (m + 1) * 128] * s for m in range(32))

    accs = lax.fori_loop(
        0, 32, weigh, tuple(jnp.zeros((8, 128), F32) for _ in range(32))
    )
    for m in range(32):
        BV[:, m * 128 : (m + 1) * 128] = accs[m]
    out = jnp.zeros((64, 1024), F32)
    for q in range(4):
        sel = jnp.zeros((64, 8), F32)
        for n in range(8):
            hit = (n8 == n) & (i64 == own[n] * 8 + rank[n] * 4 + q)
            sel = sel + jnp.where(hit, 1.0, 0.0)
        out = out + jnp.dot(
            sel.astype(BF), BV[:, q * 1024 : (q + 1) * 1024].astype(BF), preferred_element_type=F32
        )
    for o in range(8):
        SB[o] = out[o * 8 : (o + 1) * 8, :].astype(BF)
    keep, cs = to_owners(SB, RB, lsem.at[3])
    t64 = iota((8, 64), 0).astype(F32)
    l64 = jnp.bitwise_and(iota((8, 64), 1), 3)
    keep.wait()
    for c in cs:
        c.wait_recv()
    arrived = jnp.concatenate([RB[o].astype(F32) for o in range(8)], axis=0).astype(BF)
    for q in range(4):
        place = jnp.where((labels == t64 + 1.0) & (l64 == q), 1.0, 0.0).astype(BF)
        d = jnp.dot(place, arrived, preferred_element_type=F32)
        for m in range(8):
            FL[(q * 8 + m) * 8 : (q * 8 + m + 1) * 8, :] = d[:, m * 128 : (m + 1) * 128]
    rows_from_tiles(FL, ROWS)
    deriv = jnp.concatenate([ROWS[0], ROWS[1]], axis=1).astype(BF)

    order4 = {"+": (0, 1, 2, 3), "-": (2, 3, 0, 1)}
    def partial(i):
        return lax.dot_general(
            VIRT[pl.ds(pl.multiple_of(i * 256, 256), 256), :], deriv,
            (((1,), (1,)), ((), ())), preferred_element_type=F32,
        )

    IL = {"O": 0, "P": 1}
    ID = {"+": 0, "-": 1}
    fs = {}
    def hop(st, L, d, k, got=None):
        i, j, s = IL[L], ID[d], SIGN[d]
        h = order4[d][k]
        v = FP[base[L] + zat(st * s), h * 64 : (h + 1) * 64, :]
        if got is not None:
            fs[L, d, st + 1, k].wait_recv()
            v = v + RR[st, i, j, k].astype(F32)
        SS[st - 1, i, j, k] = v.astype(BF)
        to = shift("z", NZ, z, s)
        if st == 1 and L == "P":
            to["ylo"] = 1 - yl
        fs[L, d, st, k] = send(SS.at[st - 1, i, j, k], RR.at[st - 1, i, j, k], **to)

    def hops(st, ks, got):
        for k in ks:
            for L in "PO":
                for d in "+-":
                    hop(st, L, d, k, got)

    def fill(dist):
        for L in "PO":
            FP[base[L] + zat(dist)] = partial(base[L] + zat(dist))

    fill(4)
    hops(4, (0, 1), None)
    fill(3)
    fill(-3)
    hops(3, (2, 3), None)
    for dist in (2, -2, 1, -1, 0):
        fill(dist)
    pfwd = []
    for c, d in zip(pfar, (1, 3, 2)):
        c.wait_recv()
        o = lax.rem(yh + NYH - d, NYH) * 2 + co
        pfwd.append(send(prow(o), prow(o), **partner))
    fy = []
    for h in range(2):
        SY[h] = FP[base["P"] + z, h * 128 : (h + 1) * 128, :].astype(BF)
        fy.append(send(SY.at[h], RY.at[h], **ypair))

    hops(3, (0, 1), True)
    hops(2, (2, 3), True)
    hops(2, (0, 1), True)
    hops(1, (2, 3), True)
    hops(1, (0, 1), True)
    pown.wait()
    pcore.wait_recv()
    for c in pfwd:
        c.wait_recv()
    for c in fy:
        c.wait_recv()
    for h in (2, 3, 0, 1):
        v = FP[base["O"] + z, h * 64 : (h + 1) * 64, :]
        v = v + RY[h // 2, (h % 2) * 64 : (h % 2) * 64 + 64, :].astype(F32)
        for L in "OP":
            for d in "+-":
                k = order4[d].index(h)
                fs[L, d, 1, k].wait_recv()
                v = v + RR[0, IL[L], ID[d], k].astype(F32)
        force_out[h * 64 : (h + 1) * 64, :] = v
    for c in started:
        c.wait_send()
    assert count[0] <= NCOPY


def on_device(green_occ, green_virt, integrals, listed, metric):
    vm = pltpu.VMEM
    hbm = pl.BlockSpec(memory_space=pl.ANY)
    inv = pl.BlockSpec(memory_space=pltpu.VMEM)
    product, coeff, force = pl.pallas_call(
        body,
        out_shape=(
            jax.ShapeDtypeStruct((1024, 256), BF),
            jax.ShapeDtypeStruct((1, 32), F32),
            jax.ShapeDtypeStruct((256, 128), F32),
        ),
        in_specs=[pl.BlockSpec(memory_space=pltpu.SMEM), hbm, hbm, hbm, inv],
        out_specs=(hbm, inv, inv),
        scratch_shapes=[
            vm((4096, 256), BF),
            vm((16, 128, 256), BF),
            vm((32, 8, 4096), BF),
            vm((256, 128), F32),
            vm((2, 128, 128), F32),
            vm((128, 256), BF),
            vm((2, 1, 128), F32),
            vm((32, 1, 128), F32),
            vm((16, 1, 128), F32),
            vm((32, 8, 128), F32),
            vm((32, 128), F32),
            vm((8, 1, 128), F32),
            vm((8, 1, 128), F32),
            vm((8, 4096), F32),
            vm((8, 8, 1024), BF),
            vm((8, 8, 1024), BF),
            vm((8, 8, 1024), BF),
            vm((8, 8, 1024), BF),
            vm((16, 256, 128), F32),
            vm((4, 2, 2, 4, 64, 128), BF),
            vm((4, 2, 2, 4, 64, 128), BF),
            vm((2, 128, 128), BF),
            vm((2, 128, 128), BF),
            pltpu.SemaphoreType.DMA((NCOPY,)),
            pltpu.SemaphoreType.DMA((NCOPY,)),
            pltpu.SemaphoreType.DMA((5,)),
            pltpu.SemaphoreType.REGULAR,
        ],
        compiler_params=pltpu.CompilerParams(
            collective_id=0, has_side_effects=True, vmem_limit_bytes=60 << 20
        ),
        name="force_window",
    )(
        listed.reshape(1, 8), green_occ, green_virt, integrals.reshape(32, 8, 4096), metric
    )
    return product, coeff.reshape(32), force


def solution(mesh):
    split = Mesh(
        mesh.devices.reshape(NX, NYL, NZ, NYH, NCO), ("row", "ylo", "z", "yhi", "core")
    )
    col, aux = ("ylo", "z"), ("yhi", "core")
    return jax.shard_map(
        on_device,
        mesh=split,
        in_specs=(
            P("row", col),
            P("row", col),
            P("row", col, aux, None, None),
            P("row", col, aux, None),
            P(aux, None),
        ),
        out_specs=(P("row", col), P(aux), P(col, ("row", *aux))),
        check_vma=False,
    )
```

```python
import jax
import jax.numpy as jnp
from jax import lax
from jax.experimental import pallas as pl
from jax.experimental.pallas import tpu as pltpu
from jax.sharding import Mesh
from jax.sharding import PartitionSpec as P

MESH = pl.DeviceIdType.MESH
BF = jnp.bfloat16
F32 = jnp.float32
NX, NYL, NZ, NYH, NCO = 4, 2, 8, 4, 2
NCOPY = 208


def iota(shape, dim):
    return lax.broadcasted_iota(jnp.int32, shape, dim)


def rows_from_tiles(fl, rows):
    left = iota((32, 128), 1) < 64
    for br in range(2):
        for q in range(2):
            t = br * 4 + 2 * q
            a = fl[pl.ds(t, 32, stride=8), :]
            b = fl[pl.ds(t + 1, 32, stride=8), :]
            even = jnp.where(left, a, pltpu.roll(b, 64, 1))
            odd = jnp.where(left, pltpu.roll(a, 64, 1), b)
            rows[q, pl.ds(br * 64, 32, stride=2), :] = even
            rows[q, pl.ds(br * 64 + 1, 32, stride=2), :] = odd


def tiles_from_rows(rows, fl):
    left = iota((32, 128), 1) < 64
    for br in range(2):
        for q in range(2):
            t = br * 4 + 2 * q
            even = rows[q, pl.ds(br * 64, 32, stride=2), :]
            odd = rows[q, pl.ds(br * 64 + 1, 32, stride=2), :]
            fl[pl.ds(t, 32, stride=8), :] = jnp.where(left, even, pltpu.roll(odd, 64, 1))
            fl[pl.ds(t + 1, 32, stride=8), :] = jnp.where(left, pltpu.roll(even, 64, 1), odd)


def body(
    listed, occ, virt, ints, metric, prod_out, coeff_out, force_out,
    VIRT, OCC, AV, FL, ROWS, PR, CSRC, CZX, CY, ACC, SCB, LSRC, LB,
    BV, SB, RB, ST, RT, FP, SS, RR, SY, RY, ssem, rsem, lsem, ready,
):
    x = lax.axis_index("row")
    yl = lax.axis_index("ylo")
    z = lax.axis_index("z")
    yh = lax.axis_index("yhi")
    co = lax.axis_index("core")
    a = yh * 2 + co
    count = [0]
    started = []

    def send(src, dst, **to):
        k = count[0]
        count[0] += 1
        c = pltpu.make_async_remote_copy(
            src_ref=src, dst_ref=dst, send_sem=ssem.at[k], recv_sem=rsem.at[k],
            device_id=to, device_id_type=MESH,
        )
        c.start()
        started.append(c)
        return c

    def shift(axis, n, me, d):
        return {axis: lax.rem(me + d + n, n)}

    def ypeers():
        for dl in range(NYL):
            for dh in range(NYH):
                for dc in range(NCO):
                    if dl or dh or dc:
                        yield {
                            "ylo": lax.rem(yl + dl, NYL),
                            "yhi": lax.rem(yh + dh, NYH),
                            "core": lax.rem(co + dc, NCO),
                        }

    partner = {"core": 1 - co}
    ypair = {"ylo": 1 - yl}

    local = [
        pltpu.make_async_copy(virt, VIRT.at[pl.ds(x * 1024, 1024)], lsem.at[0]),
        pltpu.make_async_copy(occ.at[pl.ds(a * 128, 128)], OCC.at[yl * 8 + z], lsem.at[1]),
        pltpu.make_async_copy(ints, AV, lsem.at[2]),
    ]
    for c in local:
        c.start()

    barrier = pltpu.get_barrier_semaphore()
    zx = [
        {"row": lax.rem(x + dx, NX), "z": lax.rem(z + dz, NZ)}
        for dx in range(NX) for dz in range(NZ) if dx or dz
    ]
    diag = [{"ylo": 1 - yl, "z": lax.rem(z + d + NZ, NZ)} for d in (1, -1)]
    peers = [shift("row", NX, x, d) for d in (1, -1)]
    peers += [shift("z", NZ, z, d) for d in (1, -1, 2, -2)]
    peers += diag + [ypair]
    peers += [
        {"yhi": lax.rem(yh + dh, NYH), "core": lax.rem(co + dc, NCO)}
        for dh in range(NYH) for dc in range(NCO) if dh or dc
    ]
    for p in peers:
        pl.semaphore_signal(barrier, inc=1, device_id=p, device_id_type=MESH)
    pl.semaphore_wait(barrier, len(peers))

    def vq(r, half, quarter):
        return VIRT.at[pl.ds(r * 1024 + half * 512 + quarter * 256, 256)]

    def own_vq(quarter):
        return virt.at[pl.ds(co * 512 + quarter * 256, 256)]

    def xblk(d):
        return lax.rem(x + d + NX, NX)

    def occ_half(c, h):
        return OCC.at[c, pl.ds(h * 64, 64)]

    def own_half(h):
        return occ.at[pl.ds(a * 128 + h * 64, 64)]

    def zat(d):
        return lax.rem(z + d + NZ, NZ)

    SIGN = {"+": 1, "-": -1}
    cme = yl * 8 + z
    base = {"O": yl * 8, "P": (1 - yl) * 8}
    order = {"+": (0, 1), "-": (1, 0)}
    zs = {}
    zy = []
    for k in range(2):
        for L in "PO":
            for d in "+-":
                h = order[d][k]
                to = shift("z", NZ, z, SIGN[d])
                if L == "P":
                    to["ylo"] = 1 - yl
                zs[L, d, 1, h] = send(own_half(h), occ_half(cme, h), **to)
    xs = {}
    for d, quarters in (("+", (0, 1)), ("-", (1, 0))):
        xs[d] = [
            send(own_vq(q), vq(x, co, q), **shift("row", NX, x, SIGN[d])) for q in quarters
        ]
    lane = iota((8, 128), 1)
    subl = iota((8, 128), 0)
    idx = [listed[0, n] for n in range(8)]
    own = [lax.shift_right_logical(v, 3) for v in idx]
    pos = [jnp.bitwise_and(v, 7) for v in idx]
    rank = []
    for n in range(8):
        r = jnp.int32(0)
        for m in range(n):
            r = r + jnp.where(own[m] == own[n], 1, 0).astype(jnp.int32)
        rank.append(r)
    table = jnp.zeros((8, 128), F32)
    for n in range(8):
        hit = (subl == own[n]) & (lane // 4 == a * 2 + rank[n])
        table = table + jnp.where(hit, (pos[n] + 1).astype(F32), 0.0)
    for o in range(8):
        LSRC[o] = table[o : o + 1, :]
    LB[a] = LSRC[a]
    lab = []
    for dh in range(NYH):
        for dc in range(NCO):
            if dh or dc:
                h2 = lax.rem(yh + dh, NYH)
                c2 = lax.rem(co + dc, NCO)
                lab.append(send(LSRC.at[h2 * 2 + c2], LB.at[a], yhi=h2, core=c2))

    for h in range(2):
        zy.append(send(own_half(h), occ_half(cme, h), **ypair))

    def relay(step):
        for k in range(2):
            for L in "OP":
                for d in "+-":
                    s = SIGN[d]
                    h = order[d][k]
                    zs[L, d, step, h].wait_recv()
                    blk = occ_half(base[L] + zat(-s * step), h)
                    if step <= 2:
                        zs[L, d, step + 1, h] = send(blk, blk, **shift("z", NZ, z, s))
                    if step == 2 and k == 0:
                        zs[L, d, 4, h] = send(blk, blk, **shift("z", NZ, z, 2 * s))

    fwd = []

    def xfwd(r, q):
        fwd.append(send(vq(r, co, q), vq(r, co, q), **partner))

    relay(1)
    for d, q in (("+", 0), ("-", 1)):
        s = SIGN[d]
        xs[d][0].wait_recv()
        r = xblk(-s)
        xs[d].append(send(vq(r, co, q), vq(r, co, q), **shift("row", NX, x, s)))
        xfwd(r, q)
    relay(2)
    for d, q in (("+", 1), ("-", 0)):
        xs[d][1].wait_recv()
        xfwd(xblk(-SIGN[d]), q)
    for d, q in (("+", 0), ("-", 1)):
        xs[d][2].wait_recv()
        xfwd(xblk(2), q)
    for c in local[:2]:
        c.wait()
    for c in zy:
        c.wait_recv()
    for c in lab:
        c.wait_recv()
    for c in fwd:
        c.wait_recv()

    def mm(c, acc):
        return acc + jnp.dot(
            OCC[c], VIRT[pl.ds(pl.multiple_of(c * 256, 256), 256), :], preferred_element_type=F32
        )

    acc = jnp.zeros((128, 256), F32)
    for dist in (0, 1, -1, 2, -2):
        for L in "OP":
            acc = mm(base[L] + zat(dist), acc)
    relay(3)
    for dist in (3, -3):
        for L in "OP":
            acc = mm(base[L] + zat(dist), acc)
    for L in "OP":
        for d in "+-":
            zs[L, d, 4, order[d][0]].wait_recv()
        acc = mm(base[L] + zat(4), acc)
    for d in range(1, NX):
        pl.semaphore_signal(
            ready, inc=1, device_id=shift("row", NX, x, d), device_id_type=MESH
        )
    PR[...] = acc.astype(BF)
    for q in range(2):
        ROWS[q] = acc[:, q * 128 : (q + 1) * 128]
    tiles_from_rows(ROWS, FL)
    for m in range(32):
        BV[:, m * 128 : (m + 1) * 128] = FL[m * 8 : (m + 1) * 8, :]

    labels = LB[0]
    for o in range(1, 8):
        labels = labels + LB[o]
    labels = labels[:, 0:64]
    square = jnp.broadcast_to(labels, (64, 64))
    labels_down = jnp.sum(
        jnp.where(iota((64, 64), 0) == iota((64, 64), 1), square, 0.0), axis=1, keepdims=True
    )
    i64 = iota((64, 8), 0)
    n8 = iota((64, 8), 1)
    q64 = jnp.bitwise_and(i64, 3)
    out = jnp.zeros((64, 1024), F32)
    for q in range(4):
        take = jnp.where((labels_down == (n8 + 1).astype(F32)) & (q64 == q), 1.0, 0.0)
        out = out + jnp.dot(
            take.astype(BF), BV[:, q * 1024 : (q + 1) * 1024].astype(BF), preferred_element_type=F32
        )
    for o in range(8):
        ST[o] = out[o * 8 : (o + 1) * 8, :].astype(BF)

    def to_owners(src, dst, sem):
        keep = pltpu.make_async_copy(src.at[a], dst.at[a], sem)
        keep.start()
        cs = []
        for dh in (2, 1, 3, 0):
            for dc in range(NCO):
                if dh or dc:
                    h2 = lax.rem(yh + dh, NYH)
                    c2 = lax.rem(co + dc, NCO)
                    cs.append(send(src.at[h2 * 2 + c2], dst.at[a], yhi=h2, core=c2))
        return keep, cs

    keep, cs = to_owners(ST, RT, lsem.at[3])
    keep.wait()
    for c in cs:
        c.wait_recv()

    def prow(o):
        return prod_out.at[pl.ds(o * 128, 128)]

    pown = pltpu.make_async_copy(PR, prow(a), lsem.at[4])
    pown.start()
    pcore = send(PR, prow(a), **partner)
    pfar = [send(PR, prow(a), **shift("yhi", NYH, yh, d)) for d in (1, 3, 2)]

    arrived = jnp.concatenate([RT[o].astype(F32) for o in range(8)], axis=0).astype(BF)
    s64 = iota((8, 64), 1)
    n64 = iota((8, 64), 0)
    chosen = []
    for q in range(4):
        pick = jnp.zeros((8, 64), F32)
        for n in range(8):
            hit = (n64 == n) & (s64 == own[n] * 8 + rank[n] * 4 + q)
            pick = pick + jnp.where(hit, 1.0, 0.0)
        chosen.append(jnp.dot(pick.astype(BF), arrived, preferred_element_type=F32))
    chosen = jnp.concatenate(chosen, axis=1)
    local[2].wait()

    def contract(p, _):
        v = AV[p].astype(F32) * chosen
        s = v[:, 0:128]
        for m in range(1, 32):
            s = s + v[:, m * 128 : (m + 1) * 128]
        ACC[p] = s
        return 0

    lax.fori_loop(0, 32, contract, 0, unroll=2)
    part = jnp.sum(jnp.sum(ACC[...], axis=1), axis=1, keepdims=True)
    lane32 = iota((32, 128), 1)
    sub32 = iota((32, 128), 0)
    spread = jnp.where(lane32 == sub32 + lax.rem(a, 4) * 32, part, 0.0)
    spread = jnp.sum(spread, axis=0, keepdims=True)

    def exchange(k, value, buf, slot, targets):
        CSRC[k] = value
        buf[slot] = value
        for c in [send(CSRC.at[k], buf.at[slot], **t) for t in targets]:
            c.wait_recv()

    pl.semaphore_wait(ready, NX - 1)
    exchange(0, spread, CZX, x * 8 + z, zx)
    total = CZX[0]
    for i in range(1, NX * NZ):
        total = total + CZX[i]
    exchange(1, total, CY, yl * 8 + a, list(ypeers()))
    halves = []
    for first in (0, 4):
        total = CY[first]
        for i in (1, 2, 3, 8, 9, 10, 11):
            total = total + CY[first + i]
        halves.append(total)

    row = jnp.where(a // 4 == 0, halves[0], halves[1])
    mine = jnp.zeros((1, 32), F32)
    for k in range(4):
        mine = mine + jnp.where(lax.rem(a, 4) == k, row[:, k * 32 : (k + 1) * 32], 0.0)
    coeff_out[...] = mine

    scr = metric[:, 0:128] * halves[0] + metric[:, 128:256] * halves[1]
    scr = jnp.sum(scr, axis=1, keepdims=True)
    SCB[...] = jnp.broadcast_to(scr, (32, 128))

    def weigh(p, accs):
        s = SCB[pl.ds(p, 1), :]
        v = AV[p].astype(F32)
        return tuple(accs[m] + v[:, m * 128 : (m + 1) * 128] * s for m in range(32))

    accs = lax.fori_loop(
        0, 32, weigh, tuple(jnp.zeros((8, 128), F32) for _ in range(32))
    )
    for m in range(32):
        BV[:, m * 128 : (m + 1) * 128] = accs[m]
    out = jnp.zeros((64, 1024), F32)
    for q in range(4):
        sel = jnp.zeros((64, 8), F32)
        for n in range(8):
            hit = (n8 == n) & (i64 == own[n] * 8 + rank[n] * 4 + q)
            sel = sel + jnp.where(hit, 1.0, 0.0)
        out = out + jnp.dot(
            sel.astype(BF), BV[:, q * 1024 : (q + 1) * 1024].astype(BF), preferred_element_type=F32
        )
    for o in range(8):
        SB[o] = out[o * 8 : (o + 1) * 8, :].astype(BF)
    keep, cs = to_owners(SB, RB, lsem.at[3])
    t64 = iota((8, 64), 0).astype(F32)
    l64 = jnp.bitwise_and(iota((8, 64), 1), 3)
    keep.wait()
    for c in cs:
        c.wait_recv()
    arrived = jnp.concatenate([RB[o].astype(F32) for o in range(8)], axis=0).astype(BF)
    for q in range(4):
        place = jnp.where((labels == t64 + 1.0) & (l64 == q), 1.0, 0.0).astype(BF)
        d = jnp.dot(place, arrived, preferred_element_type=F32)
        for m in range(8):
            FL[(q * 8 + m) * 8 : (q * 8 + m + 1) * 8, :] = d[:, m * 128 : (m + 1) * 128]
    rows_from_tiles(FL, ROWS)
    deriv = jnp.concatenate([ROWS[0], ROWS[1]], axis=1).astype(BF)

    order4 = {"+": (0, 1, 2, 3), "-": (2, 3, 0, 1)}
    def partial(i):
        return lax.dot_general(
            VIRT[pl.ds(pl.multiple_of(i * 256, 256), 256), :], deriv,
            (((1,), (1,)), ((), ())), preferred_element_type=F32,
        )

    IL = {"O": 0, "P": 1}
    ID = {"+": 0, "-": 1}
    fs = {}
    def hop(st, L, d, k, got=None):
        i, j, s = IL[L], ID[d], SIGN[d]
        h = order4[d][k]
        v = FP[base[L] + zat(st * s), h * 64 : (h + 1) * 64, :]
        if got is not None:
            fs[L, d, st + 1, k].wait_recv()
            v = v + RR[st, i, j, k].astype(F32)
        SS[st - 1, i, j, k] = v.astype(BF)
        to = shift("z", NZ, z, s)
        if st == 1 and L == "P":
            to["ylo"] = 1 - yl
        fs[L, d, st, k] = send(SS.at[st - 1, i, j, k], RR.at[st - 1, i, j, k], **to)

    def hops(st, ks, got):
        for k in ks:
            for L in "PO":
                for d in "+-":
                    hop(st, L, d, k, got)

    def fill(dist):
        for L in "PO":
            FP[base[L] + zat(dist)] = partial(base[L] + zat(dist))

    fill(4)
    hops(4, (0, 1), None)
    fill(3)
    fill(-3)
    hops(3, (2, 3), None)
    for dist in (2, -2, 1, -1, 0):
        fill(dist)
    pfwd = []
    for c, d in zip(pfar, (1, 3, 2)):
        c.wait_recv()
        o = lax.rem(yh + NYH - d, NYH) * 2 + co
        pfwd.append(send(prow(o), prow(o), **partner))
    fy = []
    for h in range(2):
        SY[h] = FP[base["P"] + z, h * 128 : (h + 1) * 128, :].astype(BF)
        fy.append(send(SY.at[h], RY.at[h], **ypair))

    hops(3, (0, 1), True)
    hops(2, (2, 3), True)
    hops(2, (0, 1), True)
    hops(1, (2, 3), True)
    hops(1, (0, 1), True)
    pown.wait()
    pcore.wait_recv()
    for c in pfwd:
        c.wait_recv()
    for c in fy:
        c.wait_recv()
    for h in (2, 3, 0, 1):
        v = FP[base["O"] + z, h * 64 : (h + 1) * 64, :]
        v = v + RY[h // 2, (h % 2) * 64 : (h % 2) * 64 + 64, :].astype(F32)
        for L in "OP":
            for d in "+-":
                k = order4[d].index(h)
                fs[L, d, 1, k].wait_recv()
                v = v + RR[0, IL[L], ID[d], k].astype(F32)
        force_out[h * 64 : (h + 1) * 64, :] = v
    for c in started:
        c.wait_send()
    assert count[0] <= NCOPY


def hand_out(p, c, f, p_out, c_out, f_out):
    p_out[...] = p[...]
    c_out[...] = c[...]
    f_out[...] = f[...]


def on_device(green_occ, green_virt, integrals, listed, metric):
    vm = pltpu.VMEM
    hbm = pl.BlockSpec(memory_space=pl.ANY)
    inv = pl.BlockSpec(memory_space=pltpu.VMEM)
    product, coeff, force = pl.pallas_call(
        body,
        out_shape=(
            jax.ShapeDtypeStruct((1024, 256), BF),
            jax.ShapeDtypeStruct((1, 32), F32),
            jax.ShapeDtypeStruct((256, 128), F32),
        ),
        in_specs=[pl.BlockSpec(memory_space=pltpu.SMEM), hbm, hbm, hbm, inv],
        out_specs=(hbm, inv, inv),
        scratch_shapes=[
            vm((4096, 256), BF),
            vm((16, 128, 256), BF),
            vm((32, 8, 4096), BF),
            vm((256, 128), F32),
            vm((2, 128, 128), F32),
            vm((128, 256), BF),
            vm((2, 1, 128), F32),
            vm((32, 1, 128), F32),
            vm((16, 1, 128), F32),
            vm((32, 8, 128), F32),
            vm((32, 128), F32),
            vm((8, 1, 128), F32),
            vm((8, 1, 128), F32),
            vm((8, 4096), F32),
            vm((8, 8, 1024), BF),
            vm((8, 8, 1024), BF),
            vm((8, 8, 1024), BF),
            vm((8, 8, 1024), BF),
            vm((16, 256, 128), F32),
            vm((4, 2, 2, 4, 64, 128), BF),
            vm((4, 2, 2, 4, 64, 128), BF),
            vm((2, 128, 128), BF),
            vm((2, 128, 128), BF),
            pltpu.SemaphoreType.DMA((NCOPY,)),
            pltpu.SemaphoreType.DMA((NCOPY,)),
            pltpu.SemaphoreType.DMA((5,)),
            pltpu.SemaphoreType.REGULAR,
        ],
        compiler_params=pltpu.CompilerParams(
            collective_id=0, has_side_effects=True, vmem_limit_bytes=60 << 20
        ),
        name="force_window",
    )(
        listed.reshape(1, 8), green_occ, green_virt, integrals.reshape(32, 8, 4096), metric
    )
    return pl.pallas_call(
        hand_out,
        out_shape=(
            jax.ShapeDtypeStruct((1024, 256), BF),
            jax.ShapeDtypeStruct((32,), F32),
            jax.ShapeDtypeStruct((256, 128), F32),
        ),
        in_specs=[inv] * 3,
        out_specs=(inv, inv, inv),
        name="hand_out",
    )(product, coeff.reshape(32), force)


def solution(mesh):
    split = Mesh(
        mesh.devices.reshape(NX, NYL, NZ, NYH, NCO), ("row", "ylo", "z", "yhi", "core")
    )
    col, aux = ("ylo", "z"), ("yhi", "core")
    return jax.shard_map(
        on_device,
        mesh=split,
        in_specs=(
            P("row", col),
            P("row", col),
            P("row", col, aux, None, None),
            P("row", col, aux, None),
            P(aux, None),
        ),
        out_specs=(P("row", col), P(aux), P(col, ("row", *aux))),
        check_vma=False,
    )
```

```python
import jax
import jax.numpy as jnp
from jax import lax
from jax.experimental import pallas as pl
from jax.experimental.pallas import tpu as pltpu
from jax.sharding import Mesh
from jax.sharding import PartitionSpec as P

MESH = pl.DeviceIdType.MESH
BF = jnp.bfloat16
F32 = jnp.float32
NX, NYL, NZ, NYH, NCO = 4, 2, 8, 4, 2
NCOPY = 208


def iota(shape, dim):
    return lax.broadcasted_iota(jnp.int32, shape, dim)


def rows_from_tiles(fl, rows):
    left = iota((32, 128), 1) < 64
    for br in range(2):
        for q in range(2):
            t = br * 4 + 2 * q
            a = fl[pl.ds(t, 32, stride=8), :]
            b = fl[pl.ds(t + 1, 32, stride=8), :]
            even = jnp.where(left, a, pltpu.roll(b, 64, 1))
            odd = jnp.where(left, pltpu.roll(a, 64, 1), b)
            rows[q, pl.ds(br * 64, 32, stride=2), :] = even
            rows[q, pl.ds(br * 64 + 1, 32, stride=2), :] = odd


def tiles_from_rows(rows, fl):
    left = iota((32, 128), 1) < 64
    for br in range(2):
        for q in range(2):
            t = br * 4 + 2 * q
            even = rows[q, pl.ds(br * 64, 32, stride=2), :]
            odd = rows[q, pl.ds(br * 64 + 1, 32, stride=2), :]
            fl[pl.ds(t, 32, stride=8), :] = jnp.where(left, even, pltpu.roll(odd, 64, 1))
            fl[pl.ds(t + 1, 32, stride=8), :] = jnp.where(left, pltpu.roll(even, 64, 1), odd)


def body(
    listed, occ, virt, ints, metric, prod_out, coeff_out, force_out,
    VIRT, OCC, AV, FL, ROWS, PR, CSRC, CZX, CY, ACC, SCB, LSRC, LB,
    BV, SB, RB, ST, RT, FP, SS, RR, SY, RY, ssem, rsem, lsem, ready,
):
    x = lax.axis_index("row")
    yl = lax.axis_index("ylo")
    z = lax.axis_index("z")
    yh = lax.axis_index("yhi")
    co = lax.axis_index("core")
    a = yh * 2 + co
    count = [0]
    started = []

    def send(src, dst, **to):
        k = count[0]
        count[0] += 1
        c = pltpu.make_async_remote_copy(
            src_ref=src, dst_ref=dst, send_sem=ssem.at[k], recv_sem=rsem.at[k],
            device_id=to, device_id_type=MESH,
        )
        c.start()
        started.append(c)
        return c

    def shift(axis, n, me, d):
        return {axis: lax.rem(me + d + n, n)}

    def ypeers():
        for dl in range(NYL):
            for dh in range(NYH):
                for dc in range(NCO):
                    if dl or dh or dc:
                        yield {
                            "ylo": lax.rem(yl + dl, NYL),
                            "yhi": lax.rem(yh + dh, NYH),
                            "core": lax.rem(co + dc, NCO),
                        }

    partner = {"core": 1 - co}
    ypair = {"ylo": 1 - yl}

    local = [
        pltpu.make_async_copy(virt, VIRT.at[pl.ds(x * 1024, 1024)], lsem.at[0]),
        pltpu.make_async_copy(occ.at[pl.ds(a * 128, 128)], OCC.at[yl * 8 + z], lsem.at[1]),
        pltpu.make_async_copy(ints, AV, lsem.at[2]),
    ]
    for c in local:
        c.start()

    barrier = pltpu.get_barrier_semaphore()
    zx = [
        {"row": lax.rem(x + dx, NX), "z": lax.rem(z + dz, NZ)}
        for dx in range(NX) for dz in range(NZ) if dx or dz
    ]
    diag = [{"ylo": 1 - yl, "z": lax.rem(z + d + NZ, NZ)} for d in (1, -1)]
    peers = [shift("row", NX, x, d) for d in (1, -1)]
    peers += [shift("z", NZ, z, d) for d in (1, -1, 2, -2)]
    peers += diag + [ypair]
    peers += [
        {"yhi": lax.rem(yh + dh, NYH), "core": lax.rem(co + dc, NCO)}
        for dh in range(NYH) for dc in range(NCO) if dh or dc
    ]
    for p in peers:
        pl.semaphore_signal(barrier, inc=1, device_id=p, device_id_type=MESH)
    lane = iota((8, 128), 1)
    subl = iota((8, 128), 0)
    idx = [listed[0, n] for n in range(8)]
    own = [lax.shift_right_logical(v, 3) for v in idx]
    pos = [jnp.bitwise_and(v, 7) for v in idx]
    rank = []
    for n in range(8):
        r = jnp.int32(0)
        for m in range(n):
            r = r + jnp.where(own[m] == own[n], 1, 0).astype(jnp.int32)
        rank.append(r)
    table = jnp.zeros((8, 128), F32)
    for n in range(8):
        hit = (subl == own[n]) & (lane // 4 == a * 2 + rank[n])
        table = table + jnp.where(hit, (pos[n] + 1).astype(F32), 0.0)
    for o in range(8):
        LSRC[o] = table[o : o + 1, :]
    pl.semaphore_wait(barrier, len(peers))

    def vq(r, half, quarter):
        return VIRT.at[pl.ds(r * 1024 + half * 512 + quarter * 256, 256)]

    def own_vq(quarter):
        return virt.at[pl.ds(co * 512 + quarter * 256, 256)]

    def xblk(d):
        return lax.rem(x + d + NX, NX)

    def occ_half(c, h):
        return OCC.at[c, pl.ds(h * 64, 64)]

    def own_half(h):
        return occ.at[pl.ds(a * 128 + h * 64, 64)]

    def zat(d):
        return lax.rem(z + d + NZ, NZ)

    SIGN = {"+": 1, "-": -1}
    cme = yl * 8 + z
    base = {"O": yl * 8, "P": (1 - yl) * 8}
    order = {"+": (0, 1), "-": (1, 0)}
    zs = {}
    zy = []
    for k in range(2):
        for L in "PO":
            for d in "+-":
                h = order[d][k]
                to = shift("z", NZ, z, SIGN[d])
                if L == "P":
                    to["ylo"] = 1 - yl
                zs[L, d, 1, h] = send(own_half(h), occ_half(cme, h), **to)
    xs = {}
    for d, quarters in (("+", (0, 1)), ("-", (1, 0))):
        xs[d] = [
            send(own_vq(q), vq(x, co, q), **shift("row", NX, x, SIGN[d])) for q in quarters
        ]
    LB[a] = LSRC[a]
    lab = []
    for dh in range(NYH):
        for dc in range(NCO):
            if dh or dc:
                h2 = lax.rem(yh + dh, NYH)
                c2 = lax.rem(co + dc, NCO)
                lab.append(send(LSRC.at[h2 * 2 + c2], LB.at[a], yhi=h2, core=c2))

    for h in range(2):
        zy.append(send(own_half(h), occ_half(cme, h), **ypair))

    def relay(step):
        for k in range(2):
            for L in "OP":
                for d in "+-":
                    s = SIGN[d]
                    h = order[d][k]
                    zs[L, d, step, h].wait_recv()
                    blk = occ_half(base[L] + zat(-s * step), h)
                    if step <= 2:
                        zs[L, d, step + 1, h] = send(blk, blk, **shift("z", NZ, z, s))
                    if step == 2 and k == 0:
                        zs[L, d, 4, h] = send(blk, blk, **shift("z", NZ, z, 2 * s))

    fwd = []

    def xfwd(r, q):
        fwd.append(send(vq(r, co, q), vq(r, co, q), **partner))

    relay(1)
    for d, q in (("+", 0), ("-", 1)):
        s = SIGN[d]
        xs[d][0].wait_recv()
        r = xblk(-s)
        xs[d].append(send(vq(r, co, q), vq(r, co, q), **shift("row", NX, x, s)))
        xfwd(r, q)
    relay(2)
    for d, q in (("+", 1), ("-", 0)):
        xs[d][1].wait_recv()
        xfwd(xblk(-SIGN[d]), q)
    for d, q in (("+", 0), ("-", 1)):
        xs[d][2].wait_recv()
        xfwd(xblk(2), q)
    for c in local[:2]:
        c.wait()
    for c in zy:
        c.wait_recv()
    for c in lab:
        c.wait_recv()
    for c in fwd:
        c.wait_recv()

    def mm(c, acc):
        return acc + jnp.dot(
            OCC[c], VIRT[pl.ds(pl.multiple_of(c * 256, 256), 256), :], preferred_element_type=F32
        )

    acc = jnp.zeros((128, 256), F32)
    for dist in (0, 1, -1, 2, -2):
        for L in "OP":
            acc = mm(base[L] + zat(dist), acc)
    relay(3)
    for dist in (3, -3):
        for L in "OP":
            acc = mm(base[L] + zat(dist), acc)
    for L in "OP":
        for d in "+-":
            zs[L, d, 4, order[d][0]].wait_recv()
        acc = mm(base[L] + zat(4), acc)
    for d in range(1, NX):
        pl.semaphore_signal(
            ready, inc=1, device_id=shift("row", NX, x, d), device_id_type=MESH
        )
    PR[...] = acc.astype(BF)
    for q in range(2):
        ROWS[q] = acc[:, q * 128 : (q + 1) * 128]
    tiles_from_rows(ROWS, FL)
    for m in range(32):
        BV[:, m * 128 : (m + 1) * 128] = FL[m * 8 : (m + 1) * 8, :]

    labels = LB[0]
    for o in range(1, 8):
        labels = labels + LB[o]
    labels = labels[:, 0:64]
    square = jnp.broadcast_to(labels, (64, 64))
    labels_down = jnp.sum(
        jnp.where(iota((64, 64), 0) == iota((64, 64), 1), square, 0.0), axis=1, keepdims=True
    )
    i64 = iota((64, 8), 0)
    n8 = iota((64, 8), 1)
    q64 = jnp.bitwise_and(i64, 3)
    out = jnp.zeros((64, 1024), F32)
    for q in range(4):
        take = jnp.where((labels_down == (n8 + 1).astype(F32)) & (q64 == q), 1.0, 0.0)
        out = out + jnp.dot(
            take.astype(BF), BV[:, q * 1024 : (q + 1) * 1024].astype(BF), preferred_element_type=F32
        )
    for o in range(8):
        ST[o] = out[o * 8 : (o + 1) * 8, :].astype(BF)

    def to_owners(src, dst, sem):
        keep = pltpu.make_async_copy(src.at[a], dst.at[a], sem)
        keep.start()
        cs = []
        for dh in (2, 1, 3, 0):
            for dc in range(NCO):
                if dh or dc:
                    h2 = lax.rem(yh + dh, NYH)
                    c2 = lax.rem(co + dc, NCO)
                    cs.append(send(src.at[h2 * 2 + c2], dst.at[a], yhi=h2, core=c2))
        return keep, cs

    keep, cs = to_owners(ST, RT, lsem.at[3])
    keep.wait()
    for c in cs:
        c.wait_recv()

    def prow(o):
        return prod_out.at[pl.ds(o * 128, 128)]

    pown = pltpu.make_async_copy(PR, prow(a), lsem.at[4])
    pown.start()
    pcore = send(PR, prow(a), **partner)
    pfar = [send(PR, prow(a), **shift("yhi", NYH, yh, d)) for d in (1, 3, 2)]

    arrived = jnp.concatenate([RT[o].astype(F32) for o in range(8)], axis=0).astype(BF)
    s64 = iota((8, 64), 1)
    n64 = iota((8, 64), 0)
    chosen = []
    for q in range(4):
        pick = jnp.zeros((8, 64), F32)
        for n in range(8):
            hit = (n64 == n) & (s64 == own[n] * 8 + rank[n] * 4 + q)
            pick = pick + jnp.where(hit, 1.0, 0.0)
        chosen.append(jnp.dot(pick.astype(BF), arrived, preferred_element_type=F32))
    chosen = jnp.concatenate(chosen, axis=1)
    local[2].wait()

    def contract(p, _):
        v = AV[p].astype(F32) * chosen
        s = v[:, 0:128]
        for m in range(1, 32):
            s = s + v[:, m * 128 : (m + 1) * 128]
        ACC[p] = s
        return 0

    lax.fori_loop(0, 32, contract, 0, unroll=4)
    part = jnp.sum(jnp.sum(ACC[...], axis=1), axis=1, keepdims=True)
    lane32 = iota((32, 128), 1)
    sub32 = iota((32, 128), 0)
    spread = jnp.where(lane32 == sub32 + lax.rem(a, 4) * 32, part, 0.0)
    spread = jnp.sum(spread, axis=0, keepdims=True)

    def exchange(k, value, buf, slot, targets):
        CSRC[k] = value
        buf[slot] = value
        for c in [send(CSRC.at[k], buf.at[slot], **t) for t in targets]:
            c.wait_recv()

    pl.semaphore_wait(ready, NX - 1)
    exchange(0, spread, CZX, x * 8 + z, zx)
    total = CZX[0]
    for i in range(1, NX * NZ):
        total = total + CZX[i]
    exchange(1, total, CY, yl * 8 + a, list(ypeers()))
    halves = []
    for first in (0, 4):
        total = CY[first]
        for i in (1, 2, 3, 8, 9, 10, 11):
            total = total + CY[first + i]
        halves.append(total)

    row = jnp.where(a // 4 == 0, halves[0], halves[1])
    mine = jnp.zeros((1, 32), F32)
    for k in range(4):
        mine = mine + jnp.where(lax.rem(a, 4) == k, row[:, k * 32 : (k + 1) * 32], 0.0)
    coeff_out[...] = mine

    scr = metric[:, 0:128] * halves[0] + metric[:, 128:256] * halves[1]
    scr = jnp.sum(scr, axis=1, keepdims=True)
    SCB[...] = jnp.broadcast_to(scr, (32, 128))

    def weigh(p, accs):
        s = SCB[pl.ds(p, 1), :]
        v = AV[p].astype(F32)
        return tuple(accs[m] + v[:, m * 128 : (m + 1) * 128] * s for m in range(32))

    accs = lax.fori_loop(
        0, 32, weigh, tuple(jnp.zeros((8, 128), F32) for _ in range(32)), unroll=2
    )
    for m in range(32):
        BV[:, m * 128 : (m + 1) * 128] = accs[m]
    out = jnp.zeros((64, 1024), F32)
    for q in range(4):
        sel = jnp.zeros((64, 8), F32)
        for n in range(8):
            hit = (n8 == n) & (i64 == own[n] * 8 + rank[n] * 4 + q)
            sel = sel + jnp.where(hit, 1.0, 0.0)
        out = out + jnp.dot(
            sel.astype(BF), BV[:, q * 1024 : (q + 1) * 1024].astype(BF), preferred_element_type=F32
        )
    for o in range(8):
        SB[o] = out[o * 8 : (o + 1) * 8, :].astype(BF)
    keep, cs = to_owners(SB, RB, lsem.at[3])
    t64 = iota((8, 64), 0).astype(F32)
    l64 = jnp.bitwise_and(iota((8, 64), 1), 3)
    keep.wait()
    for c in cs:
        c.wait_recv()
    arrived = jnp.concatenate([RB[o].astype(F32) for o in range(8)], axis=0).astype(BF)
    for q in range(4):
        place = jnp.where((labels == t64 + 1.0) & (l64 == q), 1.0, 0.0).astype(BF)
        d = jnp.dot(place, arrived, preferred_element_type=F32)
        for m in range(8):
            FL[(q * 8 + m) * 8 : (q * 8 + m + 1) * 8, :] = d[:, m * 128 : (m + 1) * 128]
    rows_from_tiles(FL, ROWS)
    deriv = jnp.concatenate([ROWS[0], ROWS[1]], axis=1).astype(BF)

    order4 = {"+": (0, 1, 2, 3), "-": (2, 3, 0, 1)}
    def partial(i):
        return lax.dot_general(
            VIRT[pl.ds(pl.multiple_of(i * 256, 256), 256), :], deriv,
            (((1,), (1,)), ((), ())), preferred_element_type=F32,
        )

    IL = {"O": 0, "P": 1}
    ID = {"+": 0, "-": 1}
    fs = {}
    def hop(st, L, d, k, got=None):
        i, j, s = IL[L], ID[d], SIGN[d]
        h = order4[d][k]
        v = FP[base[L] + zat(st * s), h * 64 : (h + 1) * 64, :]
        if got is not None:
            fs[L, d, st + 1, k].wait_recv()
            v = v + RR[st, i, j, k].astype(F32)
        SS[st - 1, i, j, k] = v.astype(BF)
        to = shift("z", NZ, z, s)
        if st == 1 and L == "P":
            to["ylo"] = 1 - yl
        fs[L, d, st, k] = send(SS.at[st - 1, i, j, k], RR.at[st - 1, i, j, k], **to)

    def hops(st, ks, got):
        for k in ks:
            for L in "PO":
                for d in "+-":
                    hop(st, L, d, k, got)

    def fill(dist):
        for L in "PO":
            FP[base[L] + zat(dist)] = partial(base[L] + zat(dist))

    fill(4)
    hops(4, (0, 1), None)
    fill(3)
    fill(-3)
    hops(3, (2, 3), None)
    for dist in (2, -2, 1, -1, 0):
        fill(dist)
    pfwd = []
    for c, d in zip(pfar, (1, 3, 2)):
        c.wait_recv()
        o = lax.rem(yh + NYH - d, NYH) * 2 + co
        pfwd.append(send(prow(o), prow(o), **partner))
    fy = []
    for h in range(2):
        SY[h] = FP[base["P"] + z, h * 128 : (h + 1) * 128, :].astype(BF)
        fy.append(send(SY.at[h], RY.at[h], **ypair))

    hops(3, (0, 1), True)
    hops(2, (2, 3), True)
    hops(2, (0, 1), True)
    hops(1, (2, 3), True)
    hops(1, (0, 1), True)
    pown.wait()
    pcore.wait_recv()
    for c in pfwd:
        c.wait_recv()
    for c in fy:
        c.wait_recv()
    for h in (2, 3, 0, 1):
        v = FP[base["O"] + z, h * 64 : (h + 1) * 64, :]
        v = v + RY[h // 2, (h % 2) * 64 : (h % 2) * 64 + 64, :].astype(F32)
        for L in "OP":
            for d in "+-":
                k = order4[d].index(h)
                fs[L, d, 1, k].wait_recv()
                v = v + RR[0, IL[L], ID[d], k].astype(F32)
        force_out[h * 64 : (h + 1) * 64, :] = v
    for c in started:
        c.wait_send()
    assert count[0] <= NCOPY


def hand_out(p, c, f, p_out, c_out, f_out):
    p_out[...] = p[...]
    c_out[...] = c[...]
    f_out[...] = f[...]


def on_device(green_occ, green_virt, integrals, listed, metric):
    vm = pltpu.VMEM
    hbm = pl.BlockSpec(memory_space=pl.ANY)
    inv = pl.BlockSpec(memory_space=pltpu.VMEM)
    product, coeff, force = pl.pallas_call(
        body,
        out_shape=(
            jax.ShapeDtypeStruct((1024, 256), BF),
            jax.ShapeDtypeStruct((1, 32), F32),
            jax.ShapeDtypeStruct((256, 128), F32),
        ),
        in_specs=[pl.BlockSpec(memory_space=pltpu.SMEM), hbm, hbm, hbm, inv],
        out_specs=(hbm, inv, inv),
        scratch_shapes=[
            vm((4096, 256), BF),
            vm((16, 128, 256), BF),
            vm((32, 8, 4096), BF),
            vm((256, 128), F32),
            vm((2, 128, 128), F32),
            vm((128, 256), BF),
            vm((2, 1, 128), F32),
            vm((32, 1, 128), F32),
            vm((16, 1, 128), F32),
            vm((32, 8, 128), F32),
            vm((32, 128), F32),
            vm((8, 1, 128), F32),
            vm((8, 1, 128), F32),
            vm((8, 4096), F32),
            vm((8, 8, 1024), BF),
            vm((8, 8, 1024), BF),
            vm((8, 8, 1024), BF),
            vm((8, 8, 1024), BF),
            vm((16, 256, 128), F32),
            vm((4, 2, 2, 4, 64, 128), BF),
            vm((4, 2, 2, 4, 64, 128), BF),
            vm((2, 128, 128), BF),
            vm((2, 128, 128), BF),
            pltpu.SemaphoreType.DMA((NCOPY,)),
            pltpu.SemaphoreType.DMA((NCOPY,)),
            pltpu.SemaphoreType.DMA((5,)),
            pltpu.SemaphoreType.REGULAR,
        ],
        compiler_params=pltpu.CompilerParams(
            collective_id=0, has_side_effects=True, vmem_limit_bytes=60 << 20
        ),
        name="force_window",
    )(
        listed.reshape(1, 8), green_occ, green_virt, integrals.reshape(32, 8, 4096), metric
    )
    return pl.pallas_call(
        hand_out,
        out_shape=(
            jax.ShapeDtypeStruct((1024, 256), BF),
            jax.ShapeDtypeStruct((32,), F32),
            jax.ShapeDtypeStruct((256, 128), F32),
        ),
        in_specs=[inv] * 3,
        out_specs=(inv, inv, inv),
        name="hand_out",
    )(product, coeff.reshape(32), force)


def solution(mesh):
    split = Mesh(
        mesh.devices.reshape(NX, NYL, NZ, NYH, NCO), ("row", "ylo", "z", "yhi", "core")
    )
    col, aux = ("ylo", "z"), ("yhi", "core")
    return jax.shard_map(
        on_device,
        mesh=split,
        in_specs=(
            P("row", col),
            P("row", col),
            P("row", col, aux, None, None),
            P("row", col, aux, None),
            P(aux, None),
        ),
        out_specs=(P("row", col), P(aux), P(col, ("row", *aux))),
        check_vma=False,
    )
```
